256 devices in a mesh: tm: 4 (over x), area: 64 (over z, y, core).
Axes of the slice: x: 4, y: 4, z: 8, core: 2. Of those that a mesh axis runs over, the one named last changes fastest.
Arguments:
- gradient: float32 [168, 256, 512], P('tm', 'area'), may hold values from -72 to 72
- barrier: float32 [1], replicated, may hold values from 0.5 to 2
- slack: float32 [168, 256, 512], P('tm', 'area'), may hold values from 0.5 to 2
- hess_diag: float32 [168, 256, 512], P('tm', 'area'), may hold values from 0.5 to 2
- tile: float32 [256, 512, 512], P('area'), may hold values from -0.1 to 4.1, as said below
- ramp_weight: float32 [256, 512], P('area'), may hold values from 0.5 to 2
- bus_coupling: float32 [256, 512], P('area'), may hold values from 0.5 to 2
- tie_offset: int32 [256, 4], replicated, may hold values from 1 to 4, as said below
- tie_admittance: float32 [256, 4], replicated, may hold values from 0.5 to 2
- con_sens: float32 [16384, 512], P('area'), may hold values from -0.9 to 0.9
- con_weight: float32 [16384, 168], P('area', 'tm'), may hold values from 0.5 to 2
- con_owner: int32 [16384, 1], P('area'), may hold values from 0 to 255; in each aligned block of 256 rows (0 to 255, 256 to 511, ...) at most 2 rows name the same one
- step_guess: float32 [168, 256, 512], P('tm', 'area'), may hold values from -1.2 to 1.2
Outputs:
- newton_step: float32 [168, 256, 512], P('tm', 'area')
- residual: float32 [168, 256, 512], P('tm', 'area')
The draws below stay inside these ranges and needn't reach their ends.
Inputs may be any that keep to these rules, and one draw needn't show every extreme that they name: `tie_offset`: each tie partner lies 1 to 4 areas above its area; a partner past the last area is absent. `con_owner`: on the rows of one index of area, no area owns more than 2 blocks. Each area's tile is symmetric.
All inputs are finite; a program needn't handle non-finite values.
Results may differ from the reference program's by a relative error of at most 0.00028.
Values sent between devices are 32-bit elements; how exact they have to be, the bound alone decides.
A program may use at most 64 MiB of HBM per device.

```python
import math
import jax
import jax.numpy as jnp
import numpy as np
from jax import lax

NV = 512
TIES = 4
ITERS = 2
AREA_DEV = 4
NCON_DEV = 256
HOURS = 168
AREAS = 256
NCON = 16384
CAP = 2


def draw_gradient(key, part):
    area_scale = 1.0 + 2.0 * jnp.arange(AREAS, dtype=jnp.float32) / max(AREAS - 1, 1)
    values = jnp.clip(jax.random.normal(key, (HOURS, AREAS, NV), jnp.float32), -6.0, 6.0)
    return 4.0 * values * area_scale[None, :, None]


def draw_tile(key, part):
    values = jax.random.uniform(key, (AREAS, NV, NV), jnp.float32, -0.1, 0.1)
    mirrored = 0.5 * (values + jnp.swapaxes(values, 1, 2))
    return mirrored + 4.0 * jnp.eye(NV, dtype=jnp.float32)[None]


def draw_tie_offset(key, part):
    values = jax.random.randint(key, (AREAS, TIES), 1, AREA_DEV + 1, dtype=jnp.int32)
    values = values.at[0, 0].set(AREA_DEV)
    return values.at[0, 1].set(1)


def level_of(own_key, shape, split, least, high):
    factor_of = 1.0
    for dim, parts in split:
        heights = jax.random.uniform(jax.random.fold_in(jax.random.fold_in(own_key, 6), dim), (parts,), jnp.float32, least / len(split), high / len(split))
        factor_of = factor_of * jnp.repeat(jnp.exp(heights), shape[dim] // parts).reshape((-1,) + (1,) * (len(shape) - 1 - dim))
    return factor_of


def deal_out(rng, own, number, rows, amount, top, reach, skew):
    ranking = jax.random.permutation(rng, amount)
    heavy_load, usual = load_shares(amount, rows * top, reach, skew, True), load_shares(amount, rows * top, reach, skew, False)
    places = jnp.arange(amount)

    def named(tallies, rotation):
        used = int((tallies > 0).sum())
        fixed = max(1, used // 4)
        shifted = fixed + (places - fixed + rotation * (used - fixed)) % max(1, amount - fixed)
        return jnp.zeros((amount,), jnp.int32).at[ranking[jnp.where(places < fixed, places, shifted)]].set(jnp.asarray(tallies, jnp.int32))

    tallies = jnp.where(number % 4 == 0, named(heavy_load, number // 4), named(usual, number - number // 4 - 1))
    mixed = jax.random.permutation(jax.random.fold_in(own, 3), amount)
    giver, taker = mixed[0:amount // 2 * 2:2], mixed[1:amount // 2 * 2:2]
    room = jnp.minimum(tallies[giver] - 1, reach - tallies[taker]) // 2
    room = jnp.where((giver == ranking[0]) | (taker == ranking[0]) | (tallies[taker] == 0), 0, jnp.maximum(room, 0))
    shifted = jax.random.randint(jax.random.fold_in(own, 4), (amount // 2,), 0, 1 << 20) % (room + 1)
    tallies = tallies.at[giver].add(-shifted).at[taker].add(shifted)
    members = jnp.searchsorted(jnp.cumsum(tallies), jnp.arange(rows * top), side="right").astype(jnp.int32)
    table = members.reshape(top, rows).T
    table = table[jax.random.permutation(jax.random.fold_in(own, 1), rows)]
    rotation = jax.random.randint(jax.random.fold_in(own, 2), (rows, 1), 0, top)
    return jnp.take_along_axis(table, (jnp.arange(top)[None, :] + rotation) % top, axis=1)


def load_shares(count, total, bound, lean, full):
    loads = [(1 << 20) // math.isqrt(standing ** lean) + 1 for standing in range(1, count + 1)]
    largest = bound if full else min(bound, max(-(-total // count), total * loads[0] // sum(loads)))
    least = 1 if total - largest >= count - 1 else 0
    holding, spare = [largest] + [least] * (count - 1), total - largest - least * (count - 1)
    while spare > 0:
        free = [i for i in range(1, count) if holding[i] < largest] or [i for i in range(1, count) if holding[i] < bound]
        pool, remaining = sum([loads[i] for i in free]), spare
        for i in free:
            extra = min(bound - holding[i], max(1, remaining * loads[i] // pool), spare)
            holding[i] = holding[i] + extra
            spare = spare - extra
    return np.array(holding)


def bell_draw(own_key, shape, spread, bound, cuts=(), kind=jnp.bfloat16):
    drawn = jax.random.normal(own_key, shape, jnp.float32) * spread
    if len(cuts) > 0:
        drawn = level_of(own_key, shape, cuts, -0.22, 0.18) * drawn
    return jnp.clip(drawn, min=-bound, max=bound).astype(kind)


def setup_inputs(seed: int = 0) -> dict:
    streams_of = jax.random.split(jax.random.key(seed), 14)
    gradient = draw_gradient(jax.random.fold_in(streams_of[13], 71), 0)
    barrier = jnp.clip(jnp.exp(jax.random.uniform(streams_of[1], (1,), jnp.float32, math.log(0.5), math.log(2.0))), 0.5, 2.0)
    slack = jnp.clip(jnp.exp(math.log(2.0) - 1.3862944 * jax.random.uniform(streams_of[2], (HOURS, AREAS, NV), jnp.float32) ** level_of(streams_of[2], (HOURS, AREAS, NV), ((0, 4), (1, 64)), -0.2, 0.2)), 0.5, 2.0)
    hess_diag = jnp.clip(jnp.exp(math.log(2.0) - 1.3862944 * jax.random.uniform(streams_of[3], (HOURS, AREAS, NV), jnp.float32) ** level_of(streams_of[3], (HOURS, AREAS, NV), ((0, 4), (1, 64)), -0.2, 0.2)), 0.5, 2.0)
    tile = draw_tile(jax.random.fold_in(streams_of[13], 71), 0)
    ramp_weight = jnp.clip(jnp.exp(math.log(2.0) - 1.3862944 * jax.random.uniform(streams_of[5], (AREAS, NV), jnp.float32) ** level_of(streams_of[5], (AREAS, NV), ((0, 64),), -0.2, 0.2)), 0.5, 2.0)
    bus_coupling = jnp.clip(jnp.exp(math.log(2.0) - 1.3862944 * jax.random.uniform(streams_of[6], (AREAS, NV), jnp.float32) ** level_of(streams_of[6], (AREAS, NV), ((0, 64),), -0.2, 0.2)), 0.5, 2.0)
    tie_offset = draw_tie_offset(jax.random.fold_in(streams_of[13], 71), 0)
    tie_admittance = jnp.clip(jnp.exp(jax.random.uniform(streams_of[8], (AREAS, TIES), jnp.float32, math.log(0.5), math.log(2.0))), 0.5, 2.0)
    con_sens = bell_draw(streams_of[9], (NCON, NV), 0.15, 0.9, ((0, 64),), jnp.float32)
    con_weight = jnp.clip(jnp.exp(math.log(2.0) - 1.3862944 * jax.random.uniform(streams_of[10], (NCON, HOURS), jnp.float32) ** level_of(streams_of[10], (NCON, HOURS), ((0, 64), (1, 4)), -0.2, 0.2)), 0.5, 2.0)
    con_owner_keys = jax.random.split(jax.random.fold_in(streams_of[11], 1), NCON // NCON_DEV)
    con_owner_turns = jax.random.permutation(jax.random.fold_in(streams_of[11], 3), NCON // NCON_DEV)
    con_owner = jax.vmap(lambda own, number: deal_out(jax.random.fold_in(streams_of[11], 2), own, number, NCON_DEV, AREAS, 1, CAP, 2))(con_owner_keys, con_owner_turns).reshape((NCON, 1))
    step_guess = bell_draw(streams_of[12], (HOURS, AREAS, NV), 0.2, 1.2, ((0, 4), (1, 64)), jnp.float32)
    return dict(gradient=gradient, barrier=barrier, slack=slack, hess_diag=hess_diag, tile=tile, ramp_weight=ramp_weight, bus_coupling=bus_coupling, tie_offset=tie_offset, tie_admittance=tie_admittance, con_sens=con_sens, con_weight=con_weight, con_owner=con_owner, step_guess=step_guess)


def tie_product(input_vector, bus_coupling, tie_offset, tie_admittance):
    area_count = input_vector.shape[1]
    summed = jnp.zeros_like(input_vector)
    positions = jnp.arange(area_count, dtype=jnp.int32)
    for column in range(TIES):
        target = positions + tie_offset[:, column].astype(jnp.int32)
        inside = target < area_count
        clipped = jnp.minimum(target, area_count - 1).astype(jnp.int32)
        far_coupling = jnp.where(inside[:, None], bus_coupling[clipped], jnp.zeros_like(bus_coupling))
        weight = tie_admittance[:, column][:, None] * bus_coupling * far_coupling
        tie_term = weight[None] * (input_vector - input_vector[:, clipped])
        summed = summed + tie_term
        summed = summed.at[:, clipped].add(-tie_term)
    return summed


def security_product(input_vector, con_sens, con_weight, con_owner):
    blocks = con_sens.shape[0] // NCON_DEV
    sensitivity_blocks = con_sens.reshape(blocks, NCON_DEV, con_sens.shape[1])
    weight_tiles = con_weight.reshape(blocks, NCON_DEV, con_weight.shape[1])
    owner_blocks = con_owner[:, 0].astype(jnp.int32).reshape(blocks, NCON_DEV)

    def visit_block(summed, block_items):
        sensitivity, weight, owner_area = block_items
        chosen_entries = input_vector[:, owner_area, :]
        flows = jnp.einsum('tcb,cb->tc', chosen_entries, sensitivity, precision=lax.Precision.HIGHEST)
        scaled = flows * weight.T
        summed = summed.at[:, owner_area, :].add(scaled[:, :, None] * sensitivity[None])
        return summed, None

    summed, unused = lax.scan(visit_block, jnp.zeros_like(input_vector), (sensitivity_blocks, weight_tiles, owner_blocks))
    return summed


def apply_operator(input_vector, diagonal_entries, tile, ramp_weight, bus_coupling, tie_offset, tie_admittance, con_sens, con_weight, con_owner):
    operator_output = diagonal_entries * input_vector + jnp.einsum('uog,ogn->uon', input_vector, tile, precision=lax.Precision.HIGHEST)
    padded = jnp.pad(input_vector, ((1, 1), (0, 0), (0, 0)))
    operator_output = operator_output + ramp_weight[None] * (2.0 * input_vector - padded[:-2] - padded[2:])
    operator_output = operator_output + tie_product(input_vector, bus_coupling, tie_offset, tie_admittance)
    return operator_output + security_product(input_vector, con_sens, con_weight, con_owner)


def reference(gradient, barrier, slack, hess_diag, tile, ramp_weight, bus_coupling, tie_offset, tie_admittance, con_sens, con_weight, con_owner, step_guess):
    diagonal_entries = hess_diag + barrier[0] / (slack * slack)
    right_side = barrier[0] / slack - gradient

    def operate(input_vector):
        return apply_operator(input_vector, diagonal_entries, tile, ramp_weight, bus_coupling, tie_offset, tie_admittance, con_sens, con_weight, con_owner)

    solution = step_guess
    residual = right_side - operate(solution)
    search_direction = residual
    norm_now = jnp.sum(residual * residual)
    for iteration in range(ITERS):
        applied = operate(search_direction)
        step_size = norm_now / jnp.sum(search_direction * applied)
        solution = solution + step_size * search_direction
        residual = residual - step_size * applied
        if iteration + 1 < ITERS:
            norm_next = jnp.sum(residual * residual)
            search_direction = residual + (norm_next / norm_now) * search_direction
            norm_now = norm_next
    return solution, residual
```

```python
import functools

import jax
import jax.numpy as jnp
from jax import lax
from jax.experimental import pallas as pl
from jax.experimental.pallas import tpu as pltpu
from jax.sharding import PartitionSpec as P

MESH = pl.DeviceIdType.MESH
TIES = 4
HOUR_TILE = 8
Y_SIZE = 4
CORES = 2
F32 = jnp.float32
BF16 = jnp.bfloat16


def split(x):
    high = x.astype(BF16)
    return high, (x - high.astype(F32)).astype(BF16)


def product(stacked, high, right_high, right_low, dims):
    rows = high.shape[0]
    first = lax.dot_general(stacked, right_high, dims, preferred_element_type=F32)
    second = lax.dot_general(high, right_low, dims, preferred_element_type=F32)
    return first[:rows] + first[rows:] + second


NN = (((1,), (0,)), ((), ()))
NT = (((1,), (1,)), ((), ()))


def lane_sum(x):
    row = jnp.sum(x, axis=0, keepdims=True)
    width = row.shape[1]
    total = row[:, 0:128]
    for start in range(128, width, 128):
        total = total + row[:, start : start + 128]
    return total


def kernel(
    hours, tm_size, area_size,
    tie_window, diag_ref, right_ref, guess_ref, tile_hbm, ramp_ref, coup_ref, sens_hbm, weight_ref,
    step_ref, resid_ref,
    tile_buf, tile_high, tile_low, sens_buf, sens_high, sens_low,
    diag_buf, tie_buf, field, acc, halo, hour_stage, hour_halo, coup_halo,
    red_stage, red_slots,
    load_sem, halo_send, halo_recv, hour_send, hour_recv, coup_send, coup_recv, red_send, red_recv,
):
    span = guess_ref.shape[0]
    padded = guess_ref.shape[1]
    width = guess_ref.shape[2]
    me_t = lax.axis_index("tm")
    me_a = lax.axis_index("area")
    zed = lax.div(me_a, Y_SIZE * CORES)
    wye = lax.rem(lax.div(me_a, CORES), Y_SIZE)
    core = lax.rem(me_a, CORES)
    count_one = tm_size * Y_SIZE
    count_two = area_size // Y_SIZE
    mine = (me_t * Y_SIZE + wye, zed * CORES + core)
    counts = (count_one, count_two)

    def partner(stage, index):
        if stage == 0:
            t = lax.div(index, Y_SIZE)
            y = lax.rem(index, Y_SIZE)
            return (t, zed * (Y_SIZE * CORES) + y * CORES + core)
        z = lax.div(index, CORES)
        c = lax.rem(index, CORES)
        return (me_t, z * (Y_SIZE * CORES) + wye * CORES + c)

    above = (me_t, lax.rem(me_a + 1, area_size))
    below = (me_t, lax.rem(me_a + area_size - 1, area_size))
    later = (lax.rem(me_t + 1, tm_size), me_a)
    earlier = (lax.rem(me_t + tm_size - 1, tm_size), me_a)

    tile_load = pltpu.make_async_copy(tile_hbm, tile_buf, load_sem.at[0])
    tile_load.start()
    sens_load = pltpu.make_async_copy(sens_hbm, sens_buf, load_sem.at[1])
    sens_load.start()

    barrier = pltpu.get_barrier_semaphore()
    greeted = 0
    for stage in range(2):
        for d in range(1, counts[stage]):
            other = partner(stage, lax.rem(mine[stage] + d, counts[stage]))
            pl.semaphore_signal(barrier, inc=1, device_id=other, device_id_type=MESH)
            greeted += 1
    for other in (above, below):
        pl.semaphore_signal(barrier, inc=1, device_id=other, device_id_type=MESH)
        greeted += 1

    def stage_hours(phase, source):
        for i in range(span):
            hour_stage[phase, 0, i : i + 1, :] = source[i, 0:1, :]
            hour_stage[phase, 1, i : i + 1, :] = source[i, hours - 1 : hours, :]

    stage_hours(0, guess_ref)
    pl.semaphore_wait(barrier, greeted)

    def remote(source, target, send, recv, device):
        return pltpu.make_async_remote_copy(
            src_ref=source, dst_ref=target, send_sem=send, recv_sem=recv,
            device_id=device, device_id_type=MESH,
        )

    coup_copies = [
        remote(coup_ref, coup_halo.at[0], coup_send.at[0], coup_recv.at[0], above),
        remote(coup_ref, coup_halo.at[1], coup_send.at[1], coup_recv.at[1], below),
    ]
    for copy in coup_copies:
        copy.start()

    def field_copies(phase, source, i):
        return [
            remote(source.at[i], halo.at[phase, 0, i], halo_send.at[phase, 0, i], halo_recv.at[phase, 0, i], above),
            remote(source.at[i], halo.at[phase, 1, i], halo_send.at[phase, 1, i], halo_recv.at[phase, 1, i], below),
        ]

    def hour_copies(phase):
        return [
            remote(hour_stage.at[phase, 1], hour_halo.at[phase, 0], hour_send.at[phase, 0], hour_recv.at[phase, 0], later),
            remote(hour_stage.at[phase, 0], hour_halo.at[phase, 1], hour_send.at[phase, 1], hour_recv.at[phase, 1], earlier),
        ]

    flying = [[], [], []]
    for i in range(span):
        flying[0] += field_copies(0, guess_ref, i)
    flying[0] += hour_copies(0)
    for copy in flying[0]:
        copy.start()

    tile_load.wait()
    for i in range(span):
        high, low = split(tile_buf[i])
        tile_high[i] = high
        tile_low[i] = low
    sens_load.wait()
    for i in range(span):
        high, low = split(sens_buf[i])
        sens_high[i] = high
        sens_low[i] = low

    for copy in coup_copies:
        copy.wait()
    coupling = [coup_halo[0, i : i + 1, :] for i in range(span)]
    coupling += [coup_ref[i : i + 1, :] for i in range(span)]
    coupling += [coup_halo[1, i : i + 1, :] for i in range(span)]
    offsets = [o for o in range(-TIES, TIES + 1) if o != 0]
    for i in range(span):
        total = 2.0 * ramp_ref[i : i + 1, :]
        for k, o in enumerate(offsets):
            gain = tie_window[span + i, o - 1] if o > 0 else tie_window[span + i + o, -o - 1]
            row = coupling[span + i] * coupling[span + i + o] * gain
            tie_buf[i, k : k + 1, :] = row
            total = total + row
        diag_buf[i] = diag_ref[i] + total

    def local_part(value, i):
        high, low = split(value)
        stacked = jnp.concatenate([high, low], axis=0)
        result = product(stacked, high, tile_high[i], tile_low[i], NN)
        flow = product(stacked, high, sens_high[i], sens_low[i], NT) * weight_ref[i]
        flow_high, flow_low = split(flow)
        flow_stacked = jnp.concatenate([flow_high, flow_low], axis=0)
        return result + product(flow_stacked, flow_high, sens_high[i], sens_low[i], NN)

    rows = lax.broadcasted_iota(jnp.int32, (padded, width), 0)
    first_hours = me_t == 0
    last_hours = me_t == tm_size - 1

    def finish(phase, source, i):
        value = source[i]
        before = hour_halo[phase, 0, i : i + 1, :]
        before = jnp.where(first_hours, jnp.zeros_like(before), before)
        after = hour_halo[phase, 1, i : i + 1, :]
        after = jnp.where(last_hours, jnp.zeros_like(after), after)
        up = jnp.where(rows == hours - 1, after, pltpu.roll(value, padded - 1, 0))
        down = jnp.where(rows == 0, before, pltpu.roll(value, 1, 0))
        out = acc[i] + diag_buf[i] * value - ramp_ref[i : i + 1, :] * (up + down)
        for k, o in enumerate(offsets):
            j = i + o
            if j < 0:
                near = halo[phase, 0, span + j]
            elif j < span:
                near = source[j]
            else:
                near = halo[phase, 1, j - span]
            out = out - tie_buf[i, k : k + 1, :] * near
        return jnp.where(rows < hours, out, jnp.zeros_like(out))

    def start_stage(which, stage):
        copies = []
        for d in range(1, counts[stage]):
            to = lax.rem(mine[stage] + d, counts[stage])
            copy = remote(
                red_stage.at[which, stage], red_slots.at[which, stage, mine[stage]],
                red_send.at[which, stage, d], red_recv.at[which, stage, d], partner(stage, to),
            )
            copy.start()
            copies.append(copy)
        return copies

    def end_stage(which, stage, copies):
        for copy in copies:
            copy.wait()
        total = jnp.zeros((8, 128), F32)
        for s in range(counts[stage]):
            total = total + red_slots[which, stage, s]
        return total

    def begin(which, stage, tile):
        red_stage[which, stage] = tile
        red_slots[which, stage, mine[stage]] = tile
        return start_stage(which, stage)

    def pack(values):
        filled = jnp.zeros((8 - len(values), 128), F32)
        return jnp.concatenate(values + [filled], axis=0)

    def send_phase(phase, source):
        copies = []
        for i in range(span):
            copies += field_copies(phase, source, i)
        stage_hours(phase, source)
        copies += hour_copies(phase)
        for copy in copies:
            copy.start()
        flying[phase] = copies

    for i in range(span):
        acc[i] = local_part(guess_ref[i], i)
    for copy in flying[0]:
        copy.wait()
    sum_rr = jnp.zeros((1, 128), F32)
    for i in range(span):
        value = right_ref[i] - finish(0, guess_ref, i)
        field[0, i] = value
        sum_rr = sum_rr + lane_sum(value * value)
    send_phase(1, field.at[0])
    for i in range(span):
        acc[i] = local_part(field[0, i], i)
    for copy in flying[1]:
        copy.wait()
    sum_rv = jnp.zeros((1, 128), F32)
    for i in range(span):
        value = finish(1, field.at[0], i)
        field[1, i] = value
        sum_rv = sum_rv + lane_sum(value * field[0, i])
    send_phase(2, field.at[1])
    copies = begin(0, 0, pack([sum_rr, sum_rv]))
    half = span // 2
    for i in range(half):
        acc[i] = local_part(field[1, i], i)
    total = end_stage(0, 0, copies)
    copies = begin(0, 1, total)
    for i in range(half, span):
        acc[i] = local_part(field[1, i], i)
    for copy in flying[2]:
        copy.wait()
    for i in range(span):
        field[2, i] = finish(2, field.at[1], i)
    total = jnp.sum(end_stage(0, 1, copies), axis=1, keepdims=True)
    rr_zero, rv_zero = total[0:1], total[1:2]
    alpha_zero = rr_zero / rv_zero

    sums = [jnp.zeros((1, 128), F32) for _ in range(4)]
    for i in range(span):
        zero, one, two = field[0, i], field[1, i], field[2, i]
        resid = zero - alpha_zero * one
        image = one - alpha_zero * two
        field[2, i] = image
        acc[i] = resid
        sums[0] = sums[0] + lane_sum(resid * resid)
        sums[1] = sums[1] + lane_sum(resid * image)
        sums[2] = sums[2] + lane_sum(resid * one)
        sums[3] = sums[3] + lane_sum(zero * image)
    copies = begin(1, 0, pack(sums))
    total = end_stage(1, 0, copies)
    copies = begin(1, 1, total)
    total = jnp.sum(end_stage(1, 1, copies), axis=1, keepdims=True)
    beta = total[0:1] / rr_zero
    bend = total[1:2] + beta * (total[2:3] + total[3:4]) + beta * beta * rv_zero
    alpha_one = total[0:1] / bend
    for i in range(span):
        resid = acc[i]
        zero = field[0, i]
        step_ref[i] = guess_ref[i] + alpha_zero * zero + alpha_one * (resid + beta * zero)
        resid_ref[i] = resid - alpha_one * (field[2, i] + beta * field[1, i])


def newton_kernel(tie_window, diag, right, guess, tile, ramp, coup, sens, weight, hours, tm_size, area_size):
    span, padded, width = guess.shape
    slots = sens.shape[1]
    most = max(tm_size * Y_SIZE, area_size // Y_SIZE)
    vmem = pl.BlockSpec(memory_space=pltpu.VMEM)
    anywhere = pl.BlockSpec(memory_space=pl.ANY)
    dma = pltpu.SemaphoreType.DMA
    shape = jax.ShapeDtypeStruct(guess.shape, F32)
    return pl.pallas_call(
        functools.partial(kernel, hours, tm_size, area_size),
        out_shape=(shape, shape),
        in_specs=[pl.BlockSpec(memory_space=pltpu.SMEM), vmem, vmem, vmem, anywhere, vmem, vmem, anywhere, vmem],
        out_specs=(vmem, vmem),
        scratch_shapes=[
            pltpu.VMEM(tile.shape, F32), pltpu.VMEM(tile.shape, BF16), pltpu.VMEM(tile.shape, BF16),
            pltpu.VMEM(sens.shape, F32), pltpu.VMEM(sens.shape, BF16), pltpu.VMEM(sens.shape, BF16),
            pltpu.VMEM(guess.shape, F32),
            pltpu.VMEM((span, 2 * TIES, width), F32),
            pltpu.VMEM((3,) + guess.shape, F32),
            pltpu.VMEM(guess.shape, F32),
            pltpu.VMEM((3, 2) + guess.shape, F32),
            pltpu.VMEM((3, 2, span, width), F32),
            pltpu.VMEM((3, 2, span, width), F32),
            pltpu.VMEM((2, span, width), F32),
            pltpu.VMEM((2, 2, 8, 128), F32),
            pltpu.VMEM((2, 2, most, 8, 128), F32),
            dma((2,)), dma((3, 2, span)), dma((3, 2, span)), dma((3, 2)), dma((3, 2)), dma((2,)), dma((2,)),
            dma((2, 2, most)), dma((2, 2, most)),
        ],
        compiler_params=pltpu.CompilerParams(collective_id=0, has_side_effects=True, vmem_limit_bytes=60 * 1024 * 1024),
    )(tie_window, diag, right, guess, tile, ramp, coup, sens, weight)


def body(
    gradient, barrier, slack, hess_diag, tile, ramp_weight, bus_coupling, tie_offset, tie_admittance,
    con_sens, con_weight, con_owner, step_guess,
):
    hour_count, span_areas, var_width = gradient.shape
    area_total = tie_offset.shape[0]
    groups = lax.axis_size("area")
    first_area = lax.axis_index("area") * span_areas
    capacity = max(2, (2 * con_sens.shape[0] + area_total - 1) // area_total)
    owner_area = con_owner[:, 0]
    owner_marks = (owner_area[:, None] == jnp.arange(area_total, dtype=jnp.int32)[None, :]).astype(jnp.int32)
    before = jnp.cumsum(owner_marks, axis=0) - owner_marks
    slot_rank = jnp.sum(before * owner_marks, axis=1)
    slot_index = owner_area * capacity + slot_rank
    send_sens = jnp.zeros((area_total * capacity, var_width), F32).at[slot_index].set(con_sens)
    send_weight = jnp.zeros((area_total * capacity, hour_count), F32).at[slot_index].set(con_weight)
    send_sens = send_sens.reshape(groups, span_areas * capacity, var_width)
    send_weight = send_weight.reshape(groups, span_areas * capacity, hour_count)
    got_sens = lax.all_to_all(send_sens, "area", split_axis=0, concat_axis=0, tiled=True)
    got_weight = lax.all_to_all(send_weight, "area", split_axis=0, concat_axis=0, tiled=True)
    padded = -(-hour_count // HOUR_TILE) * HOUR_TILE
    fill = ((0, 0), (0, padded - hour_count), (0, 0))
    slots = groups * capacity
    owned_sens = jnp.transpose(
        got_sens.reshape(groups, span_areas, capacity, var_width), (1, 0, 2, 3)
    ).reshape(span_areas, slots, var_width)
    owned_weight = jnp.transpose(
        got_weight.reshape(groups, span_areas, capacity, hour_count), (1, 3, 0, 2)
    ).reshape(span_areas, hour_count, slots)
    owned_weight = jnp.pad(owned_weight, fill)

    def by_area(x):
        return jnp.pad(jnp.transpose(x, (1, 0, 2)), fill)

    diag = by_area(hess_diag + barrier[0] / (slack * slack))
    right = by_area(barrier[0] / slack - gradient)
    guess = by_area(step_guess)

    reach = jnp.arange(1, TIES + 1, dtype=jnp.int32)
    inside = (jnp.arange(area_total, dtype=jnp.int32)[:, None] + reach[None, :]) < area_total
    gains = jnp.sum(
        jnp.where(tie_offset[:, :, None] == reach[None, None, :], tie_admittance[:, :, None], 0.0), axis=1
    )
    gains = jnp.where(inside, gains, 0.0)
    gains = jnp.concatenate([jnp.zeros((span_areas, TIES), F32), gains], axis=0)
    tie_window = lax.dynamic_slice(gains, (first_area, jnp.int32(0)), (2 * span_areas, TIES))

    step, residual = newton_kernel(
        tie_window, diag, right, guess, tile, ramp_weight, bus_coupling, owned_sens, owned_weight,
        hour_count, lax.axis_size("tm"), groups,
    )
    return (
        jnp.transpose(step[:, :hour_count], (1, 0, 2)),
        jnp.transpose(residual[:, :hour_count], (1, 0, 2)),
    )


def solution(mesh):
    placed = (
        P("tm", "area", None), P(), P("tm", "area", None), P("tm", "area", None), P("area", None, None),
        P("area", None), P("area", None), P(), P(), P("area", None), P("area", "tm"), P("area", None),
        P("tm", "area", None),
    )
    return jax.shard_map(
        body, mesh=mesh, in_specs=placed,
        out_specs=(P("tm", "area", None), P("tm", "area", None)), check_vma=False,
    )
```

```python
import functools

import jax
import jax.numpy as jnp
from jax import lax
from jax.experimental import pallas as pl
from jax.experimental.pallas import tpu as pltpu
from jax.sharding import PartitionSpec as P

MESH = pl.DeviceIdType.MESH
TIES = 4
CAPACITY = 2
Y_SIZE = 4
CORES = 2
F32 = jnp.float32
BF16 = jnp.bfloat16


def split(x):
    high = x.astype(BF16)
    return high, (x - high.astype(F32)).astype(BF16)


def product(stacked, high, right_high, right_low, dims):
    rows = high.shape[0]
    first = lax.dot_general(stacked, right_high, dims, preferred_element_type=F32)
    second = lax.dot_general(high, right_low, dims, preferred_element_type=F32)
    return first[:rows] + first[rows:] + second


NN = (((1,), (0,)), ((), ()))
NT = (((1,), (1,)), ((), ()))


def lane_sum(x):
    row = jnp.sum(x, axis=0, keepdims=True)
    width = row.shape[1]
    total = row[:, 0:128]
    for start in range(128, width, 128):
        total = total + row[:, start : start + 128]
    return total


def kernel(
    hours, tm_size, area_size,
    barrier_ref, tie_offset, tie_gain, slack_hbm, hess_hbm, grad_hbm, guess_hbm, tile_hbm, ramp_ref, coup_ref,
    sens_hbm, load_hbm, owner_ref,
    step_ref, resid_ref,
    raw, guess_ref, right_ref, diag_buf, tile_buf, tile_high, tile_low,
    sens_own, load_own, load_stack, sens_out, load_out, sens_got, load_got, sens_high, sens_low, weight_ref,
    tie_buf, field, acc, halo, hour_stage, hour_halo, coup_halo, red_stage, red_slots,
    load_sem, halo_send, halo_recv, hour_send, hour_recv, coup_send, coup_recv, red_send, red_recv,
    sens_send, sens_recv, load_send, load_recv, pass_send, pass_recv, relay_send,
):
    span, padded, width = guess_ref.shape
    parts = width // 128
    plane = Y_SIZE * CORES
    zeds = area_size // plane
    per_device = span * CAPACITY
    me_t = lax.axis_index("tm")
    me_a = lax.axis_index("area")
    zed = lax.div(me_a, plane)
    place = lax.rem(me_a, plane)
    wye = lax.div(place, CORES)
    core = lax.rem(place, CORES)
    count_one = tm_size * Y_SIZE
    count_two = area_size // Y_SIZE
    mine = (me_t * Y_SIZE + wye, zed * CORES + core)
    counts = (count_one, count_two)

    def partner(stage, index):
        if stage == 0:
            t = lax.div(index, Y_SIZE)
            y = lax.rem(index, Y_SIZE)
            return (t, zed * plane + y * CORES + core)
        z = lax.div(index, CORES)
        c = lax.rem(index, CORES)
        return (me_t, z * plane + wye * CORES + c)

    above = (me_t, lax.rem(me_a + 1, area_size))
    below = (me_t, lax.rem(me_a + area_size - 1, area_size))
    later = (lax.rem(me_t + 1, tm_size), me_a)
    earlier = (lax.rem(me_t + tm_size - 1, tm_size), me_a)

    quarter = pl.multiple_of(me_t * 128, 128)
    sens_load = pltpu.make_async_copy(sens_hbm.at[:, pl.ds(quarter, 128)], sens_own, load_sem.at[0])
    load_load = pltpu.make_async_copy(load_hbm, load_own, load_sem.at[1])
    raw_loads = [
        pltpu.make_async_copy(source, raw.at[k], load_sem.at[2 + k])
        for k, source in enumerate((guess_hbm, slack_hbm, hess_hbm, grad_hbm))
    ]
    tile_load = pltpu.make_async_copy(tile_hbm, tile_buf, load_sem.at[6])
    for copy in [sens_load, load_load] + raw_loads + [tile_load]:
        copy.start()

    barrier = pltpu.get_barrier_semaphore()
    greeted = 0
    for d in range(1, area_size):
        other = (me_t, lax.rem(me_a + d, area_size))
        pl.semaphore_signal(barrier, inc=1, device_id=other, device_id_type=MESH)
        greeted += 1
    for dt in range(1, tm_size):
        for y in range(Y_SIZE):
            other = (lax.rem(me_t + dt, tm_size), zed * plane + y * CORES + core)
            pl.semaphore_signal(barrier, inc=1, device_id=other, device_id_type=MESH)
            greeted += 1

    rows_held = sens_own.shape[0]
    areas = area_size * span
    owner = jnp.broadcast_to(owner_ref[...], (areas, rows_held))
    marks = jnp.where(owner == lax.broadcasted_iota(jnp.int32, owner.shape, 0), 1.0, 0.0)
    earlier_row = lax.broadcasted_iota(jnp.int32, (rows_held, rows_held), 0)
    this_row = lax.broadcasted_iota(jnp.int32, (rows_held, rows_held), 1)
    order = jnp.where(earlier_row < this_row, 1.0, 0.0).astype(BF16)
    marks_low = marks.astype(BF16)
    ahead = jnp.dot(marks_low, order, preferred_element_type=F32)
    rank = jnp.sum(ahead * marks, axis=0, keepdims=True)
    slot = owner_ref[...] * CAPACITY + rank.astype(jnp.int32)
    slots = areas * CAPACITY
    wide = jnp.broadcast_to(slot, (slots, rows_held))
    pick = jnp.where(wide == lax.broadcasted_iota(jnp.int32, wide.shape, 0), 1.0, 0.0).astype(BF16)

    def thirds(x):
        high = x.astype(BF16)
        rest = x - high.astype(F32)
        middle = rest.astype(BF16)
        return high, middle, (rest - middle.astype(F32)).astype(BF16)

    sens_load.wait()
    moved = [jnp.dot(pick, part, preferred_element_type=F32) for part in thirds(sens_own[...])]
    sens_out[...] = (moved[0] + moved[1] + moved[2]).reshape(area_size, per_device, 128)
    load_load.wait()
    loads = load_own[...]
    load_stack[...] = jnp.zeros_like(load_stack)
    load_stack[0:hours, :] = jnp.where(rank < 0.5, loads, 0.0)
    load_stack[64 : 64 + hours, :] = jnp.where(rank > 0.5, loads, 0.0)
    moved = [
        lax.dot_general(marks_low, part, NT, preferred_element_type=F32) for part in thirds(load_stack[...])
    ]
    load_out[...] = (moved[0] + moved[1] + moved[2]).reshape(area_size, span, 128)

    pl.semaphore_wait(barrier, greeted)

    def remote(source, target, send, recv, device):
        return pltpu.make_async_remote_copy(
            src_ref=source, dst_ref=target, send_sem=send, recv_sem=recv,
            device_id=device, device_id_type=MESH,
        )

    steps = [0]
    for d in range(1, (zeds + 1) // 2):
        steps += [d, -d]
    if zeds % 2 == 0:
        steps += [zeds // 2]
    steps = [d % zeds for d in steps]
    own_rows = pl.ds(pl.multiple_of(me_a * per_device, per_device), per_device)
    block_copies, load_copies = {}, {}
    for dz in steps:
        for e in range(plane):
            to = lax.rem(zed + dz, zeds) * plane + lax.rem(place + e, plane)
            key = ((zeds - dz) % zeds) * plane + (plane - e) % plane
            if dz == 0 and e == 0:
                block = pltpu.make_async_copy(sens_out.at[me_a], sens_got.at[me_t, own_rows], sens_recv.at[key])
                load = pltpu.make_async_copy(load_out.at[me_a], load_got.at[me_a], load_recv.at[key])
            else:
                block = remote(
                    sens_out.at[to], sens_got.at[me_t, own_rows], sens_send.at[key], sens_recv.at[key], (me_t, to)
                )
                load = remote(load_out.at[to], load_got.at[me_a], load_send.at[key], load_recv.at[key], (me_t, to))
            block.start()
            load.start()
            block_copies[key] = block
            load_copies[key] = load

    coup_copies = [
        remote(coup_ref, coup_halo.at[0], coup_send.at[0], coup_recv.at[0], above),
        remote(coup_ref, coup_halo.at[1], coup_send.at[1], coup_recv.at[1], below),
    ]
    for copy in coup_copies:
        copy.start()

    def piece(i, j):
        return pl.ds(j * span + i, hours, stride=span * parts)

    def columns(j):
        return slice(j * 128, (j + 1) * 128)

    raw_loads[0].wait()
    for i in range(span):
        guess_ref[i, padded - 8 : padded, :] = jnp.zeros((8, width), F32)
        for j in range(parts):
            guess_ref[i, 0:hours, columns(j)] = raw[0, piece(i, j), :]

    def stage_hours(phase, source):
        for i in range(span):
            hour_stage[phase, 0, i : i + 1, :] = source[i, 0:1, :]
            hour_stage[phase, 1, i : i + 1, :] = source[i, hours - 1 : hours, :]

    stage_hours(0, guess_ref)

    def field_copies(phase, source, i):
        return [
            remote(source.at[i], halo.at[phase, 0, i], halo_send.at[phase, 0, i], halo_recv.at[phase, 0, i], above),
            remote(source.at[i], halo.at[phase, 1, i], halo_send.at[phase, 1, i], halo_recv.at[phase, 1, i], below),
        ]

    def hour_copies(phase):
        return [
            remote(hour_stage.at[phase, 1], hour_halo.at[phase, 0], hour_send.at[phase, 0], hour_recv.at[phase, 0], later),
            remote(hour_stage.at[phase, 0], hour_halo.at[phase, 1], hour_send.at[phase, 1], hour_recv.at[phase, 1], earlier),
        ]

    flying = [[], [], []]
    for i in range(span):
        flying[0] += field_copies(0, guess_ref, i)
    flying[0] += hour_copies(0)
    for copy in flying[0]:
        copy.start()

    for copy in raw_loads[1:]:
        copy.wait()
    scale = barrier_ref[0]
    for i in range(span):
        diag_buf[i, padded - 8 : padded, :] = jnp.zeros((8, width), F32)
        right_ref[i, padded - 8 : padded, :] = jnp.zeros((8, width), F32)
        for j in range(parts):
            slack = raw[1, piece(i, j), :]
            diag_buf[i, 0:hours, columns(j)] = raw[2, piece(i, j), :] + scale / (slack * slack)
            right_ref[i, 0:hours, columns(j)] = scale / slack - raw[3, piece(i, j), :]

    tile_load.wait()
    for i in range(span):
        high, low = split(tile_buf[i])
        tile_high[i] = high
        tile_low[i] = low

    first = me_a * span

    def gains_of(start, valid):
        table = []
        for r in range(span):
            area = start + r
            row = []
            for o in range(1, TIES + 1):
                total = jnp.float32(0.0)
                for k in range(TIES):
                    total = total + jnp.where(tie_offset[k, area] == o, tie_gain[k, area], 0.0)
                inside = jnp.logical_and(valid, area + o < areas)
                row.append(jnp.where(inside, total, 0.0))
            table.append(row)
        return table

    lower_start = lax.rem(me_a + area_size - 1, area_size) * span
    window = gains_of(lower_start, me_a > 0) + gains_of(first, me_a >= 0)

    for copy in coup_copies:
        copy.wait()
    coupling = [coup_halo[0, i : i + 1, :] for i in range(span)]
    coupling += [coup_ref[i : i + 1, :] for i in range(span)]
    coupling += [coup_halo[1, i : i + 1, :] for i in range(span)]
    offsets = [o for o in range(-TIES, TIES + 1) if o != 0]
    for i in range(span):
        total = 2.0 * ramp_ref[i : i + 1, :]
        for k, o in enumerate(offsets):
            gain = window[span + i][o - 1] if o > 0 else window[span + i + o][-o - 1]
            row = coupling[span + i] * coupling[span + i + o] * gain
            tie_buf[i, k : k + 1, :] = row
            total = total + row
        diag_buf[i] = diag_buf[i] + total

    def tile_part(value, i):
        high, low = split(value)
        stacked = jnp.concatenate([high, low], axis=0)
        return product(stacked, high, tile_high[i], tile_low[i], NN)

    def security_part(value, i):
        high, low = split(value)
        stacked = jnp.concatenate([high, low], axis=0)
        flow = product(stacked, high, sens_high[i], sens_low[i], NT) * weight_ref[i]
        flow_high, flow_low = split(flow)
        flow_stacked = jnp.concatenate([flow_high, flow_low], axis=0)
        return product(flow_stacked, flow_high, sens_high[i], sens_low[i], NN)

    def local_part(value, i):
        return tile_part(value, i) + security_part(value, i)

    for i in range(span):
        acc[i] = tile_part(guess_ref[i], i)

    group = plane * per_device
    passes, relays = [], []

    def group_rows(k):
        z = lax.rem(zed + steps[k], zeds)
        return pl.ds(pl.multiple_of(z * group, group), group)

    def relay(k):
        forward = k % 2 == 0
        passes[k][0 if forward else 1].wait_recv()
        origin = lax.rem(me_t + (tm_size - 1 if forward else 1), tm_size)
        there = sens_got.at[origin, group_rows(k)]
        copy = remote(there, there, relay_send.at[k], pass_recv.at[k, 2], later if forward else earlier)
        copy.start()
        relays.append(copy)

    for k in range(zeds):
        for e in range(plane):
            key = steps[k] * plane + e
            if key == 0:
                block_copies[key].wait()
            else:
                block_copies[key].wait_recv()
        here = sens_got.at[me_t, group_rows(k)]
        pair = [
            remote(here, here, pass_send.at[k, 0], pass_recv.at[k, 0], later),
            remote(here, here, pass_send.at[k, 1], pass_recv.at[k, 1], earlier),
        ]
        for copy in pair:
            copy.start()
        passes.append(pair)
        if k >= 1:
            relay(k - 1)
    relay(zeds - 1)
    for key, copy in load_copies.items():
        if key == 0:
            copy.wait()
        else:
            copy.wait_recv()
    for i in range(span):
        seen = load_got[:, i, :].T
        weight_ref[i] = jnp.concatenate([seen[0:padded], seen[64 : 64 + padded]], axis=1)
    for k in range(zeds):
        passes[k][1 if k % 2 == 0 else 0].wait_recv()
        relays[k].wait_recv()
    for i in range(span):
        for q in range(parts):
            for c in range(CAPACITY):
                high, low = split(sens_got[q, pl.ds(i * CAPACITY + c, area_size, stride=per_device), :])
                sens_high[i, c * area_size : (c + 1) * area_size, columns(q)] = high
                sens_low[i, c * area_size : (c + 1) * area_size, columns(q)] = low

    rows = lax.broadcasted_iota(jnp.int32, (padded, width), 0)
    first_hours = me_t == 0
    last_hours = me_t == tm_size - 1

    def finish(phase, source, i):
        value = source[i]
        before = hour_halo[phase, 0, i : i + 1, :]
        before = jnp.where(first_hours, jnp.zeros_like(before), before)
        after = hour_halo[phase, 1, i : i + 1, :]
        after = jnp.where(last_hours, jnp.zeros_like(after), after)
        up = jnp.where(rows == hours - 1, after, pltpu.roll(value, padded - 1, 0))
        down = jnp.where(rows == 0, before, pltpu.roll(value, 1, 0))
        out = acc[i] + diag_buf[i] * value - ramp_ref[i : i + 1, :] * (up + down)
        for k, o in enumerate(offsets):
            j = i + o
            if j < 0:
                near = halo[phase, 0, span + j]
            elif j < span:
                near = source[j]
            else:
                near = halo[phase, 1, j - span]
            out = out - tie_buf[i, k : k + 1, :] * near
        return jnp.where(rows < hours, out, jnp.zeros_like(out))

    def start_stage(which, stage):
        copies = []
        for d in range(1, counts[stage]):
            to = lax.rem(mine[stage] + d, counts[stage])
            copy = remote(
                red_stage.at[which, stage], red_slots.at[which, stage, mine[stage]],
                red_send.at[which, stage, d], red_recv.at[which, stage, d], partner(stage, to),
            )
            copy.start()
            copies.append(copy)
        return copies

    def end_stage(which, stage, copies):
        for copy in copies:
            copy.wait()
        total = jnp.zeros((8, 128), F32)
        for s in range(counts[stage]):
            total = total + red_slots[which, stage, s]
        return total

    def begin(which, stage, tile):
        red_stage[which, stage] = tile
        red_slots[which, stage, mine[stage]] = tile
        return start_stage(which, stage)

    def pack(values):
        filled = jnp.zeros((8 - len(values), 128), F32)
        return jnp.concatenate(values + [filled], axis=0)

    def send_phase(phase, source):
        copies = []
        for i in range(span):
            copies += field_copies(phase, source, i)
        stage_hours(phase, source)
        copies += hour_copies(phase)
        for copy in copies:
            copy.start()
        flying[phase] = copies

    for i in range(span):
        acc[i] = acc[i] + security_part(guess_ref[i], i)
    for copy in flying[0]:
        copy.wait()
    sum_rr = jnp.zeros((1, 128), F32)
    for i in range(span):
        value = right_ref[i] - finish(0, guess_ref, i)
        field[0, i] = value
        sum_rr = sum_rr + lane_sum(value * value)
    send_phase(1, field.at[0])
    for i in range(span):
        acc[i] = local_part(field[0, i], i)
    for copy in flying[1]:
        copy.wait()
    sum_rv = jnp.zeros((1, 128), F32)
    for i in range(span):
        value = finish(1, field.at[0], i)
        field[1, i] = value
        sum_rv = sum_rv + lane_sum(value * field[0, i])
    send_phase(2, field.at[1])
    copies = begin(0, 0, pack([sum_rr, sum_rv]))
    half = span // 2
    for i in range(half):
        acc[i] = local_part(field[1, i], i)
    total = end_stage(0, 0, copies)
    copies = begin(0, 1, total)
    for i in range(half, span):
        acc[i] = local_part(field[1, i], i)
    for copy in flying[2]:
        copy.wait()
    for i in range(span):
        field[2, i] = finish(2, field.at[1], i)
    total = jnp.sum(end_stage(0, 1, copies), axis=1, keepdims=True)
    rr_zero, rv_zero = total[0:1], total[1:2]
    alpha_zero = rr_zero / rv_zero

    sums = [jnp.zeros((1, 128), F32) for _ in range(4)]
    for i in range(span):
        zero, one, two = field[0, i], field[1, i], field[2, i]
        resid = zero - alpha_zero * one
        image = one - alpha_zero * two
        field[2, i] = image
        acc[i] = resid
        sums[0] = sums[0] + lane_sum(resid * resid)
        sums[1] = sums[1] + lane_sum(resid * image)
        sums[2] = sums[2] + lane_sum(resid * one)
        sums[3] = sums[3] + lane_sum(zero * image)
    copies = begin(1, 0, pack(sums))
    total = end_stage(1, 0, copies)
    copies = begin(1, 1, total)
    total = jnp.sum(end_stage(1, 1, copies), axis=1, keepdims=True)
    beta = total[0:1] / rr_zero
    bend = total[1:2] + beta * (total[2:3] + total[3:4]) + beta * beta * rv_zero
    alpha_one = total[0:1] / bend
    for i in range(span):
        resid = acc[i]
        zero = field[0, i]
        step = guess_ref[i] + alpha_zero * zero + alpha_one * (resid + beta * zero)
        final = resid - alpha_one * (field[2, i] + beta * field[1, i])
        for j in range(parts):
            step_ref[piece(i, j), :] = step[0:hours, columns(j)]
            resid_ref[piece(i, j), :] = final[0:hours, columns(j)]
    for key in range(1, area_size):
        block_copies[key].wait_send()
        load_copies[key].wait_send()
    for k in range(zeds):
        for copy in passes[k]:
            copy.wait_send()
        relays[k].wait_send()


def body(
    gradient, barrier, slack, hess_diag, tile, ramp_weight, bus_coupling, tie_offset, tie_admittance,
    con_sens, con_weight, con_owner, step_guess,
):
    hours, span, width = gradient.shape
    tm_size, area_size = lax.axis_size("tm"), lax.axis_size("area")
    rows_held = con_sens.shape[0]
    parts = width // 128
    padded = -(-hours // 8) * 8
    per_device = span * CAPACITY
    zeds = area_size // (Y_SIZE * CORES)
    most = max(tm_size * Y_SIZE, area_size // Y_SIZE)
    own_slots = area_size * CAPACITY

    def rows_of(x):
        return jnp.transpose(x.reshape(hours, span, parts, 128), (0, 2, 1, 3)).reshape(hours * parts * span, 128)

    def field_of(x):
        return jnp.transpose(x.reshape(hours, parts, span, 128), (0, 2, 1, 3)).reshape(hours, span, width)

    vmem = pl.BlockSpec(memory_space=pltpu.VMEM)
    smem = pl.BlockSpec(memory_space=pltpu.SMEM)
    anywhere = pl.BlockSpec(memory_space=pl.ANY)
    dma = pltpu.SemaphoreType.DMA
    flat = jax.ShapeDtypeStruct((hours * parts * span, 128), F32)
    block = (span, padded, width)
    step, residual = pl.pallas_call(
        functools.partial(kernel, hours, tm_size, area_size),
        out_shape=(flat, flat),
        in_specs=[smem] * 3 + [anywhere] * 5 + [vmem] * 2 + [anywhere] * 2 + [vmem],
        out_specs=(vmem, vmem),
        scratch_shapes=[
            pltpu.VMEM((4,) + flat.shape, F32),
            pltpu.VMEM(block, F32), pltpu.VMEM(block, F32), pltpu.VMEM(block, F32),
            pltpu.VMEM(tile.shape, F32), pltpu.VMEM(tile.shape, BF16), pltpu.VMEM(tile.shape, BF16),
            pltpu.VMEM((rows_held, 128), F32), pltpu.VMEM((hours, rows_held), F32), pltpu.VMEM((128, rows_held), F32),
            pltpu.VMEM((area_size, per_device, 128), F32), pltpu.VMEM((area_size, span, 128), F32),
            pltpu.VMEM((parts, area_size * per_device, 128), F32), pltpu.VMEM((area_size, span, 128), F32),
            pltpu.VMEM((span, own_slots, width), BF16), pltpu.VMEM((span, own_slots, width), BF16),
            pltpu.VMEM((span, padded, own_slots), F32),
            pltpu.VMEM((span, 2 * TIES, width), F32),
            pltpu.VMEM((3,) + block, F32),
            pltpu.VMEM(block, F32),
            pltpu.VMEM((3, 2) + block, F32),
            pltpu.VMEM((3, 2, span, width), F32), pltpu.VMEM((3, 2, span, width), F32), pltpu.VMEM((2, span, width), F32),
            pltpu.VMEM((2, 2, 8, 128), F32), pltpu.VMEM((2, 2, most, 8, 128), F32),
            dma((7,)), dma((3, 2, span)), dma((3, 2, span)), dma((3, 2)), dma((3, 2)), dma((2,)), dma((2,)),
            dma((2, 2, most)), dma((2, 2, most)),
            dma((area_size,)), dma((area_size,)), dma((area_size,)), dma((area_size,)),
            dma((zeds, 2)), dma((zeds, 3)), dma((zeds,)),
        ],
        compiler_params=pltpu.CompilerParams(collective_id=0, has_side_effects=True, vmem_limit_bytes=60 * 1024 * 1024),
    )(
        barrier, tie_offset.T, tie_admittance.T, rows_of(slack), rows_of(hess_diag), rows_of(gradient),
        rows_of(step_guess), tile, ramp_weight, bus_coupling, con_sens, con_weight.T, con_owner.T,
    )
    return field_of(step), field_of(residual)


def solution(mesh):
    placed = (
        P("tm", "area", None), P(), P("tm", "area", None), P("tm", "area", None), P("area", None, None),
        P("area", None), P("area", None), P(), P(), P("area", None), P("area", "tm"), P("area", None),
        P("tm", "area", None),
    )
    return jax.shard_map(
        body, mesh=mesh, in_specs=placed,
        out_specs=(P("tm", "area", None), P("tm", "area", None)), check_vma=False,
    )
```

```python
import functools

import jax
import jax.numpy as jnp
from jax import lax
from jax.experimental import pallas as pl
from jax.experimental.pallas import tpu as pltpu
from jax.sharding import PartitionSpec as P

MESH = pl.DeviceIdType.MESH
TIES = 4
CAPACITY = 2
Y_SIZE = 4
CORES = 2
F32 = jnp.float32
BF16 = jnp.bfloat16


def split(x):
    high = x.astype(BF16)
    return high, (x - high.astype(F32)).astype(BF16)


def product(stacked, high, right_high, right_low, dims):
    rows = high.shape[0]
    first = lax.dot_general(stacked, right_high, dims, preferred_element_type=F32)
    second = lax.dot_general(high, right_low, dims, preferred_element_type=F32)
    return first[:rows] + first[rows:] + second


NN = (((1,), (0,)), ((), ()))
NT = (((1,), (1,)), ((), ()))


def lane_sum(x):
    row = jnp.sum(x, axis=0, keepdims=True)
    width = row.shape[1]
    total = row[:, 0:128]
    for start in range(128, width, 128):
        total = total + row[:, start : start + 128]
    return total


def kernel(
    hours, tm_size, area_size,
    barrier_ref, tie_offset, tie_gain, slack_hbm, hess_hbm, grad_hbm, guess_hbm, tile_hbm, ramp_ref, coup_ref,
    sens_hbm, load_hbm, owner_ref,
    step_ref, resid_ref,
    raw, guess_ref, right_ref, diag_buf, tile_buf, tile_high, tile_low,
    sens_own, load_own, load_stack, sens_out, load_out, sens_got, load_got, sens_high, sens_low, weight_ref,
    tie_buf, field, acc, halo, hour_stage, hour_halo, coup_halo, red_stage, red_slots,
    load_sem, halo_send, halo_recv, hour_send, hour_recv, coup_send, coup_recv, red_send, red_recv,
    sens_send, sens_recv, load_send, load_recv, pass_send, pass_recv, relay_send,
):
    span, padded, width = guess_ref.shape
    parts = width // 128
    plane = Y_SIZE * CORES
    zeds = area_size // plane
    per_device = span * CAPACITY
    me_t = lax.axis_index("tm")
    me_a = lax.axis_index("area")
    zed = lax.div(me_a, plane)
    place = lax.rem(me_a, plane)
    wye = lax.div(place, CORES)
    core = lax.rem(place, CORES)
    count_one = tm_size * Y_SIZE
    count_two = area_size // Y_SIZE
    mine = (me_t * Y_SIZE + wye, zed * CORES + core)
    counts = (count_one, count_two)

    def partner(stage, index):
        if stage == 0:
            t = lax.div(index, Y_SIZE)
            y = lax.rem(index, Y_SIZE)
            return (t, zed * plane + y * CORES + core)
        z = lax.div(index, CORES)
        c = lax.rem(index, CORES)
        return (me_t, z * plane + wye * CORES + c)

    above = (me_t, lax.rem(me_a + 1, area_size))
    below = (me_t, lax.rem(me_a + area_size - 1, area_size))
    later = (lax.rem(me_t + 1, tm_size), me_a)
    earlier = (lax.rem(me_t + tm_size - 1, tm_size), me_a)

    quarter = pl.multiple_of(me_t * 128, 128)
    sens_load = pltpu.make_async_copy(sens_hbm.at[:, pl.ds(quarter, 128)], sens_own, load_sem.at[0])
    load_load = pltpu.make_async_copy(load_hbm, load_own, load_sem.at[1])
    raw_loads = [
        pltpu.make_async_copy(source, raw.at[k], load_sem.at[2 + k])
        for k, source in enumerate((guess_hbm, slack_hbm, hess_hbm, grad_hbm))
    ]
    tile_load = pltpu.make_async_copy(tile_hbm, tile_buf, load_sem.at[6])
    for copy in [sens_load, load_load] + raw_loads + [tile_load]:
        copy.start()

    barrier = pltpu.get_barrier_semaphore()
    greeted = 0
    for d in range(1, area_size):
        other = (me_t, lax.rem(me_a + d, area_size))
        pl.semaphore_signal(barrier, inc=1, device_id=other, device_id_type=MESH)
        greeted += 1
    for dt in range(1, tm_size):
        for y in range(Y_SIZE):
            other = (lax.rem(me_t + dt, tm_size), zed * plane + y * CORES + core)
            pl.semaphore_signal(barrier, inc=1, device_id=other, device_id_type=MESH)
            greeted += 1

    rows_held = sens_own.shape[0]
    areas = area_size * span
    owner = jnp.broadcast_to(owner_ref[...], (areas, rows_held))
    marks = jnp.where(owner == lax.broadcasted_iota(jnp.int32, owner.shape, 0), 1.0, 0.0)
    earlier_row = lax.broadcasted_iota(jnp.int32, (rows_held, rows_held), 0)
    this_row = lax.broadcasted_iota(jnp.int32, (rows_held, rows_held), 1)
    order = jnp.where(earlier_row < this_row, 1.0, 0.0).astype(BF16)
    marks_low = marks.astype(BF16)
    ahead = jnp.dot(marks_low, order, preferred_element_type=F32)
    rank = jnp.sum(ahead * marks, axis=0, keepdims=True)
    slot = owner_ref[...] * CAPACITY + rank.astype(jnp.int32)
    slots = areas * CAPACITY
    wide = jnp.broadcast_to(slot, (slots, rows_held))
    pick = jnp.where(wide == lax.broadcasted_iota(jnp.int32, wide.shape, 0), 1.0, 0.0).astype(BF16)

    def thirds(x):
        high = x.astype(BF16)
        rest = x - high.astype(F32)
        middle = rest.astype(BF16)
        return high, middle, (rest - middle.astype(F32)).astype(BF16)

    sens_load.wait()
    moved = [jnp.dot(pick, part, preferred_element_type=F32) for part in thirds(sens_own[...])]
    sens_out[...] = (moved[0] + moved[1] + moved[2]).reshape(area_size, per_device, 128)
    load_load.wait()
    loads = load_own[...]
    load_stack[...] = jnp.zeros_like(load_stack)
    load_stack[0:hours, :] = jnp.where(rank < 0.5, loads, 0.0)
    load_stack[64 : 64 + hours, :] = jnp.where(rank > 0.5, loads, 0.0)
    moved = [
        lax.dot_general(marks_low, part, NT, preferred_element_type=F32) for part in thirds(load_stack[...])
    ]
    load_out[...] = (moved[0] + moved[1] + moved[2]).reshape(area_size, span, 128)

    pl.semaphore_wait(barrier, greeted)

    def remote(source, target, send, recv, device):
        return pltpu.make_async_remote_copy(
            src_ref=source, dst_ref=target, send_sem=send, recv_sem=recv,
            device_id=device, device_id_type=MESH,
        )

    steps = [0]
    for d in range(1, (zeds + 1) // 2):
        steps += [d, -d]
    if zeds % 2 == 0:
        steps += [zeds // 2]
    steps = [d % zeds for d in steps]
    own_rows = pl.ds(pl.multiple_of(me_a * per_device, per_device), per_device)
    block_copies, load_copies = {}, {}
    for dz in steps:
        for e in range(plane):
            to = lax.rem(zed + dz, zeds) * plane + lax.rem(place + e, plane)
            key = ((zeds - dz) % zeds) * plane + (plane - e) % plane
            if dz == 0 and e == 0:
                block = pltpu.make_async_copy(sens_out.at[me_a], sens_got.at[me_t, own_rows], sens_recv.at[key])
                load = pltpu.make_async_copy(load_out.at[me_a], load_got.at[me_a], load_recv.at[key])
            else:
                block = remote(
                    sens_out.at[to], sens_got.at[me_t, own_rows], sens_send.at[key], sens_recv.at[key], (me_t, to)
                )
                load = remote(load_out.at[to], load_got.at[me_a], load_send.at[key], load_recv.at[key], (me_t, to))
            block.start()
            block_copies[key] = block
            load_copies[key] = load

    for copy in load_copies.values():
        copy.start()
    coup_copies = [
        remote(coup_ref, coup_halo.at[0], coup_send.at[0], coup_recv.at[0], above),
        remote(coup_ref, coup_halo.at[1], coup_send.at[1], coup_recv.at[1], below),
    ]
    for copy in coup_copies:
        copy.start()

    def piece(i, j):
        return pl.ds(j * span + i, hours, stride=span * parts)

    def columns(j):
        return slice(j * 128, (j + 1) * 128)

    raw_loads[0].wait()
    for i in range(span):
        guess_ref[i, padded - 8 : padded, :] = jnp.zeros((8, width), F32)
        for j in range(parts):
            guess_ref[i, 0:hours, columns(j)] = raw[0, piece(i, j), :]

    def stage_hours(phase, source):
        for i in range(span):
            hour_stage[phase, 0, i : i + 1, :] = source[i, 0:1, :]
            hour_stage[phase, 1, i : i + 1, :] = source[i, hours - 1 : hours, :]

    def send_area(phase, source, side, i):
        copy = remote(
            source.at[i], halo.at[phase, side, i], halo_send.at[phase, side, i], halo_recv.at[phase, side, i],
            below if side else above,
        )
        copy.start()
        flying[phase][side, i] = copy

    def hour_copies(phase):
        return [
            remote(hour_stage.at[phase, 1], hour_halo.at[phase, 0], hour_send.at[phase, 0], hour_recv.at[phase, 0], later),
            remote(hour_stage.at[phase, 0], hour_halo.at[phase, 1], hour_send.at[phase, 1], hour_recv.at[phase, 1], earlier),
        ]

    def send_hours(phase, source):
        stage_hours(phase, source)
        for side, copy in enumerate(hour_copies(phase)):
            copy.start()
            flying[phase]["hours", side] = copy

    ready = (1, 2, 0, 3)
    sends = {1: [(1, 1)], 2: [(0, 2), (0, 1), (1, 2)], 0: [(1, 0)], 3: [(0, 3), (0, 0), (1, 3)]}
    flying = [{}, {}, {}]
    send_hours(0, guess_ref)
    for i in ready:
        for side, j in sends[i]:
            send_area(0, guess_ref, side, j)

    for copy in raw_loads[1:]:
        copy.wait()
    scale = barrier_ref[0]
    for i in range(span):
        diag_buf[i, padded - 8 : padded, :] = jnp.zeros((8, width), F32)
        right_ref[i, padded - 8 : padded, :] = jnp.zeros((8, width), F32)
        for j in range(parts):
            slack = raw[1, piece(i, j), :]
            diag_buf[i, 0:hours, columns(j)] = raw[2, piece(i, j), :] + scale / (slack * slack)
            right_ref[i, 0:hours, columns(j)] = scale / slack - raw[3, piece(i, j), :]

    tile_load.wait()
    for i in range(span):
        high, low = split(tile_buf[i])
        tile_high[i] = high
        tile_low[i] = low

    first = me_a * span

    def gains_of(start, valid):
        table = []
        for r in range(span):
            area = start + r
            row = []
            for o in range(1, TIES + 1):
                total = jnp.float32(0.0)
                for k in range(TIES):
                    total = total + jnp.where(tie_offset[k, area] == o, tie_gain[k, area], 0.0)
                inside = jnp.logical_and(valid, area + o < areas)
                row.append(jnp.where(inside, total, 0.0))
            table.append(row)
        return table

    lower_start = lax.rem(me_a + area_size - 1, area_size) * span
    window = gains_of(lower_start, me_a > 0) + gains_of(first, me_a >= 0)

    for copy in coup_copies:
        copy.wait()
    coupling = [coup_halo[0, i : i + 1, :] for i in range(span)]
    coupling += [coup_ref[i : i + 1, :] for i in range(span)]
    coupling += [coup_halo[1, i : i + 1, :] for i in range(span)]
    offsets = [o for o in range(-TIES, TIES + 1) if o != 0]
    for i in range(span):
        total = 2.0 * ramp_ref[i : i + 1, :]
        for k, o in enumerate(offsets):
            gain = window[span + i][o - 1] if o > 0 else window[span + i + o][-o - 1]
            row = coupling[span + i] * coupling[span + i + o] * gain
            tie_buf[i, k : k + 1, :] = row
            total = total + row
        diag_buf[i] = diag_buf[i] + total

    def tile_part(value, i):
        high, low = split(value)
        stacked = jnp.concatenate([high, low], axis=0)
        return product(stacked, high, tile_high[i], tile_low[i], NN)

    def security_part(value, i):
        high, low = split(value)
        stacked = jnp.concatenate([high, low], axis=0)
        flow = product(stacked, high, sens_high[i], sens_low[i], NT) * weight_ref[i]
        flow_high, flow_low = split(flow)
        flow_stacked = jnp.concatenate([flow_high, flow_low], axis=0)
        return product(flow_stacked, flow_high, sens_high[i], sens_low[i], NN)

    def local_part(value, i):
        return tile_part(value, i) + security_part(value, i)

    rows = lax.broadcasted_iota(jnp.int32, (padded, width), 0)
    first_hours = me_t == 0
    last_hours = me_t == tm_size - 1

    def near_part(source, i):
        value = source[i]
        beside = pltpu.roll(value, padded - 1, 0) + pltpu.roll(value, 1, 0)
        beside = jnp.where(rows < hours, beside, jnp.zeros_like(beside))
        out = acc[i] + diag_buf[i] * value - ramp_ref[i : i + 1, :] * beside
        for k, o in enumerate(offsets):
            if 0 <= i + o < span:
                out = out - tie_buf[i, k : k + 1, :] * source[i + o]
        acc[i] = out

    def hour_part(phase):
        for side in range(2):
            flying[phase]["hours", side].wait_recv()
        for i in range(span):
            ramp = ramp_ref[i : i + 1, :]
            before = ramp * hour_halo[phase, 0, i : i + 1, :]
            after = ramp * hour_halo[phase, 1, i : i + 1, :]
            acc[i, 0:1, :] = acc[i, 0:1, :] - jnp.where(first_hours, jnp.zeros_like(before), before)
            acc[i, hours - 1 : hours, :] = acc[i, hours - 1 : hours, :] - jnp.where(
                last_hours, jnp.zeros_like(after), after
            )

    def halo_part(phase, pieces):
        for piece_key in pieces:
            flying[phase][piece_key].wait_recv()
        for i in range(span):
            terms = []
            for side, j in pieces:
                o = span + j - i if side else j - span - i
                if abs(o) <= TIES:
                    k = offsets.index(o)
                    terms.append(tie_buf[i, k : k + 1, :] * halo[phase, side, j])
            if terms:
                acc[i] = acc[i] - functools.reduce(lambda x, y: x + y, terms)

    pieces_one = [(0, 2), (1, 1)]
    pieces_two = [(0, 1), (1, 2)]
    pieces_three = [(0, 3), (1, 0)]
    pieces_four = [(0, 0), (1, 3)]

    for i in range(span):
        acc[i] = tile_part(guess_ref[i], i)
        near_part(guess_ref, i)

    group = plane * per_device
    passes, relays = [], []

    def group_rows(k):
        z = lax.rem(zed + steps[k], zeds)
        return pl.ds(pl.multiple_of(z * group, group), group)

    def relay(k):
        forward = k % 2 == 0
        passes[k][0 if forward else 1].wait_recv()
        origin = lax.rem(me_t + (tm_size - 1 if forward else 1), tm_size)
        there = sens_got.at[origin, group_rows(k)]
        copy = remote(there, there, relay_send.at[k], pass_recv.at[k, 2], later if forward else earlier)
        copy.start()
        relays.append(copy)

    for k in range(zeds):
        for e in range(plane):
            key = steps[k] * plane + e
            if key == 0:
                block_copies[key].wait()
            else:
                block_copies[key].wait_recv()
        here = sens_got.at[me_t, group_rows(k)]
        pair = [
            remote(here, here, pass_send.at[k, 0], pass_recv.at[k, 0], later),
            remote(here, here, pass_send.at[k, 1], pass_recv.at[k, 1], earlier),
        ]
        for copy in pair:
            copy.start()
        passes.append(pair)
        if k >= 1:
            relay(k - 1)
    relay(zeds - 1)
    for key, copy in load_copies.items():
        if key == 0:
            copy.wait()
        else:
            copy.wait_recv()
    for i in range(span):
        seen = load_got[:, i, :].T
        weight_ref[i] = jnp.concatenate([seen[0:padded], seen[64 : 64 + padded]], axis=1)
    def place_columns(origin):
        where = pl.ds(pl.multiple_of(origin * 128, 128), 128)
        for i in range(span):
            for c in range(CAPACITY):
                high, low = split(sens_got[origin, pl.ds(i * CAPACITY + c, area_size, stride=per_device), :])
                sens_high[i, c * area_size : (c + 1) * area_size, where] = high
                sens_low[i, c * area_size : (c + 1) * area_size, where] = low

    place_columns(me_t)
    hour_part(0)
    for pieces in (pieces_one, pieces_two, pieces_three, pieces_four):
        halo_part(0, pieces)
    for k in range(zeds):
        passes[k][1 if k % 2 == 0 else 0].wait_recv()
    place_columns(lax.rem(me_t + tm_size - 1, tm_size))
    place_columns(lax.rem(me_t + 1, tm_size))
    for k in range(zeds):
        relays[k].wait_recv()
    place_columns(lax.rem(me_t + 2, tm_size))

    def start_stage(which, stage):
        copies = []
        for d in range(1, counts[stage]):
            to = lax.rem(mine[stage] + d, counts[stage])
            copy = remote(
                red_stage.at[which, stage], red_slots.at[which, stage, mine[stage]],
                red_send.at[which, stage, d], red_recv.at[which, stage, d], partner(stage, to),
            )
            copy.start()
            copies.append(copy)
        return copies

    def end_stage(which, stage, copies):
        for copy in copies:
            copy.wait()
        total = jnp.zeros((1, 128), F32)
        for s in range(counts[stage]):
            total = total + red_slots[which, stage, s]
        return total

    def begin(which, stage, tile):
        red_stage[which, stage] = tile
        red_slots[which, stage, mine[stage]] = tile
        return start_stage(which, stage)

    lanes = lax.broadcasted_iota(jnp.int32, (1, 128), 1)

    def pack(values):
        total = jnp.zeros((1, 128), F32)
        for k, value in enumerate(values):
            total = jnp.where(lanes == k, jnp.sum(value, axis=1, keepdims=True), total)
        return total

    def take(total, k):
        return jnp.sum(jnp.where(lanes == k, total, jnp.zeros_like(total)), axis=1, keepdims=True)

    sum_rr = jnp.zeros((1, 128), F32)
    for i in ready:
        value = right_ref[i] - (acc[i] + security_part(guess_ref[i], i))
        field[0, i] = value
        for side, j in sends[i]:
            send_area(1, field.at[0], side, j)
        sum_rr = sum_rr + lane_sum(value * value)
    send_hours(1, field.at[0])
    for i in ready:
        acc[i] = local_part(field[0, i], i)
        near_part(field.at[0], i)
    sum_rv = jnp.zeros((1, 128), F32)
    halo_part(1, pieces_one)
    halo_part(1, pieces_two)
    hour_part(1)
    halo_part(1, pieces_three)
    for i in ready[:2]:
        field[1, i] = acc[i]
        for side, j in sends[i]:
            send_area(2, field.at[1], side, j)
    for i in ready[:2]:
        sum_rv = sum_rv + lane_sum(field[1, i] * field[0, i])
    acc[ready[0]] = local_part(field[1, ready[0]], ready[0])
    for piece_key in pieces_four:
        flying[1][piece_key].wait_recv()
    for i, (side, j) in zip(ready[2:], pieces_four):
        k = offsets.index(span + j - i if side else j - span - i)
        field[1, i] = acc[i] - tie_buf[i, k : k + 1, :] * halo[1, side, j]
        for side, j in sends[i]:
            send_area(2, field.at[1], side, j)
    send_hours(2, field.at[1])
    for i in ready[2:]:
        sum_rv = sum_rv + lane_sum(field[1, i] * field[0, i])
    copies = begin(0, 0, pack([sum_rr, sum_rv]))
    for i in ready[1:3]:
        acc[i] = local_part(field[1, i], i)
    total = end_stage(0, 0, copies)
    copies = begin(0, 1, total)
    acc[ready[3]] = local_part(field[1, ready[3]], ready[3])
    for i in ready:
        near_part(field.at[1], i)
    halo_part(2, pieces_one)
    halo_part(2, pieces_two)
    total = end_stage(0, 1, copies)
    rr_zero, rv_zero = take(total, 0), take(total, 1)
    alpha_zero = rr_zero / rv_zero
    for i in ready:
        right_ref[i] = guess_ref[i] + alpha_zero * field[0, i]
    hour_part(2)
    halo_part(2, pieces_three)

    sums = [jnp.zeros((1, 128), F32) for _ in range(4)]
    for i in ready:
        if i == ready[2]:
            halo_part(2, pieces_four)
        zero, one, two = field[0, i], field[1, i], acc[i]
        resid = zero - alpha_zero * one
        image = one - alpha_zero * two
        field[2, i] = image
        acc[i] = resid
        sums[0] = sums[0] + lane_sum(resid * resid)
        sums[1] = sums[1] + lane_sum(resid * image)
        sums[2] = sums[2] + lane_sum(resid * one)
        sums[3] = sums[3] + lane_sum(zero * image)
    copies = begin(1, 0, pack(sums))
    total = end_stage(1, 0, copies)
    copies = begin(1, 1, total)
    total = end_stage(1, 1, copies)
    rr_one = take(total, 0)
    beta = rr_one / rr_zero
    bend = take(total, 1) + beta * (take(total, 2) + take(total, 3)) + beta * beta * rv_zero
    alpha_one = rr_one / bend
    for i in range(span):
        resid = acc[i]
        zero = field[0, i]
        step = right_ref[i] + alpha_one * (resid + beta * zero)
        final = resid - alpha_one * (field[2, i] + beta * field[1, i])
        for j in range(parts):
            step_ref[piece(i, j), :] = step[0:hours, columns(j)]
            resid_ref[piece(i, j), :] = final[0:hours, columns(j)]
    for key in range(1, area_size):
        block_copies[key].wait_send()
        load_copies[key].wait_send()
    for k in range(zeds):
        for copy in passes[k]:
            copy.wait_send()
        relays[k].wait_send()
    for group_copies in flying:
        for copy in group_copies.values():
            copy.wait_send()


def body(
    gradient, barrier, slack, hess_diag, tile, ramp_weight, bus_coupling, tie_offset, tie_admittance,
    con_sens, con_weight, con_owner, step_guess,
):
    hours, span, width = gradient.shape
    tm_size, area_size = lax.axis_size("tm"), lax.axis_size("area")
    rows_held = con_sens.shape[0]
    parts = width // 128
    padded = -(-hours // 8) * 8
    per_device = span * CAPACITY
    zeds = area_size // (Y_SIZE * CORES)
    most = max(tm_size * Y_SIZE, area_size // Y_SIZE)
    own_slots = area_size * CAPACITY

    def rows_of(x):
        return jnp.transpose(x.reshape(hours, span, parts, 128), (0, 2, 1, 3)).reshape(hours * parts * span, 128)

    def field_of(x):
        return jnp.transpose(x.reshape(hours, parts, span, 128), (0, 2, 1, 3)).reshape(hours, span, width)

    vmem = pl.BlockSpec(memory_space=pltpu.VMEM)
    smem = pl.BlockSpec(memory_space=pltpu.SMEM)
    anywhere = pl.BlockSpec(memory_space=pl.ANY)
    dma = pltpu.SemaphoreType.DMA
    flat = jax.ShapeDtypeStruct((hours * parts * span, 128), F32)
    block = (span, padded, width)
    step, residual = pl.pallas_call(
        functools.partial(kernel, hours, tm_size, area_size),
        out_shape=(flat, flat),
        in_specs=[smem] * 3 + [anywhere] * 5 + [vmem] * 2 + [anywhere] * 2 + [vmem],
        out_specs=(vmem, vmem),
        scratch_shapes=[
            pltpu.VMEM((4,) + flat.shape, F32),
            pltpu.VMEM(block, F32), pltpu.VMEM(block, F32), pltpu.VMEM(block, F32),
            pltpu.VMEM(tile.shape, F32), pltpu.VMEM(tile.shape, BF16), pltpu.VMEM(tile.shape, BF16),
            pltpu.VMEM((rows_held, 128), F32), pltpu.VMEM((hours, rows_held), F32), pltpu.VMEM((128, rows_held), F32),
            pltpu.VMEM((area_size, per_device, 128), F32), pltpu.VMEM((area_size, span, 128), F32),
            pltpu.VMEM((parts, area_size * per_device, 128), F32), pltpu.VMEM((area_size, span, 128), F32),
            pltpu.VMEM((span, own_slots, width), BF16), pltpu.VMEM((span, own_slots, width), BF16),
            pltpu.VMEM((span, padded, own_slots), F32),
            pltpu.VMEM((span, 2 * TIES, width), F32),
            pltpu.VMEM((3,) + block, F32),
            pltpu.VMEM(block, F32),
            pltpu.VMEM((3, 2) + block, F32),
            pltpu.VMEM((3, 2, span, width), F32), pltpu.VMEM((3, 2, span, width), F32), pltpu.VMEM((2, span, width), F32),
            pltpu.VMEM((2, 2, 1, 128), F32), pltpu.VMEM((2, 2, most, 1, 128), F32),
            dma((7,)), dma((3, 2, span)), dma((3, 2, span)), dma((3, 2)), dma((3, 2)), dma((2,)), dma((2,)),
            dma((2, 2, most)), dma((2, 2, most)),
            dma((area_size,)), dma((area_size,)), dma((area_size,)), dma((area_size,)),
            dma((zeds, 2)), dma((zeds, 3)), dma((zeds,)),
        ],
        compiler_params=pltpu.CompilerParams(collective_id=0, has_side_effects=True, vmem_limit_bytes=60 * 1024 * 1024),
    )(
        barrier, tie_offset.T, tie_admittance.T, rows_of(slack), rows_of(hess_diag), rows_of(gradient),
        rows_of(step_guess), tile, ramp_weight, bus_coupling, con_sens, con_weight.T, con_owner.T,
    )
    return field_of(step), field_of(residual)


def solution(mesh):
    placed = (
        P("tm", "area", None), P(), P("tm", "area", None), P("tm", "area", None), P("area", None, None),
        P("area", None), P("area", None), P(), P(), P("area", None), P("area", "tm"), P("area", None),
        P("tm", "area", None),
    )
    return jax.shard_map(
        body, mesh=mesh, in_specs=placed,
        out_specs=(P("tm", "area", None), P("tm", "area", None)), check_vma=False,
    )
```

```python
import functools

import jax
import jax.numpy as jnp
from jax import lax
from jax.experimental import pallas as pl
from jax.experimental.pallas import tpu as pltpu
from jax.sharding import PartitionSpec as P

MESH = pl.DeviceIdType.MESH
TIES = 4
CAPACITY = 2
Y_SIZE = 4
CORES = 2
F32 = jnp.float32
BF16 = jnp.bfloat16


def split(x):
    high = x.astype(BF16)
    return high, (x - high.astype(F32)).astype(BF16)


def product(stacked, high, right_high, right_low, dims):
    rows = high.shape[0]
    first = lax.dot_general(stacked, right_high, dims, preferred_element_type=F32)
    second = lax.dot_general(high, right_low, dims, preferred_element_type=F32)
    return first[:rows] + first[rows:] + second


NN = (((1,), (0,)), ((), ()))
NT = (((1,), (1,)), ((), ()))


def lane_sum(x):
    row = jnp.sum(x, axis=0, keepdims=True)
    width = row.shape[1]
    total = row[:, 0:128]
    for start in range(128, width, 128):
        total = total + row[:, start : start + 128]
    return total


def kernel(
    hours, tm_size, area_size,
    barrier_ref, tie_offset, tie_gain, slack_hbm, hess_hbm, grad_hbm, guess_hbm, tile_hbm, ramp_ref, coup_ref,
    sens_hbm, load_hbm, owner_ref,
    step_ref, resid_ref,
    raw, guess_ref, right_ref, diag_buf, tile_buf, tile_high, tile_low,
    sens_own, load_own, load_stack, sens_out, load_out, sens_got, load_got, sens_high, sens_low, weight_ref,
    tie_buf, field, acc, halo, hour_stage, hour_halo, coup_halo, red_stage, red_slots,
    load_sem, halo_send, halo_recv, hour_send, hour_recv, coup_send, coup_recv, red_send, red_recv,
    sens_send, sens_recv, load_send, load_recv, pass_send, pass_recv, relay_send,
):
    span, padded, width = guess_ref.shape
    parts = width // 128
    plane = Y_SIZE * CORES
    zeds = area_size // plane
    per_device = span * CAPACITY
    me_t = lax.axis_index("tm")
    me_a = lax.axis_index("area")
    zed = lax.div(me_a, plane)
    place = lax.rem(me_a, plane)
    wye = lax.div(place, CORES)
    core = lax.rem(place, CORES)
    count_one = tm_size * Y_SIZE
    count_two = area_size // Y_SIZE
    mine = (me_t * Y_SIZE + wye, zed * CORES + core)
    counts = (count_one, count_two)

    def partner(stage, index):
        if stage == 0:
            t = lax.div(index, Y_SIZE)
            y = lax.rem(index, Y_SIZE)
            return (t, zed * plane + y * CORES + core)
        z = lax.div(index, CORES)
        c = lax.rem(index, CORES)
        return (me_t, z * plane + wye * CORES + c)

    above = (me_t, lax.rem(me_a + 1, area_size))
    below = (me_t, lax.rem(me_a + area_size - 1, area_size))
    later = (lax.rem(me_t + 1, tm_size), me_a)
    earlier = (lax.rem(me_t + tm_size - 1, tm_size), me_a)

    quarter = pl.multiple_of(me_t * 128, 128)
    sens_load = pltpu.make_async_copy(sens_hbm.at[:, pl.ds(quarter, 128)], sens_own, load_sem.at[0])
    load_load = pltpu.make_async_copy(load_hbm, load_own, load_sem.at[1])
    raw_loads = [
        pltpu.make_async_copy(source, raw.at[k], load_sem.at[2 + k])
        for k, source in enumerate((guess_hbm, slack_hbm, hess_hbm, grad_hbm))
    ]
    tile_load = pltpu.make_async_copy(tile_hbm, tile_buf, load_sem.at[6])
    for copy in [sens_load, load_load] + raw_loads + [tile_load]:
        copy.start()

    barrier = pltpu.get_barrier_semaphore()
    greeted = 0
    for d in range(1, area_size):
        other = (me_t, lax.rem(me_a + d, area_size))
        pl.semaphore_signal(barrier, inc=1, device_id=other, device_id_type=MESH)
        greeted += 1
    for dt in range(1, tm_size):
        for y in range(Y_SIZE):
            other = (lax.rem(me_t + dt, tm_size), zed * plane + y * CORES + core)
            pl.semaphore_signal(barrier, inc=1, device_id=other, device_id_type=MESH)
            greeted += 1

    rows_held = sens_own.shape[0]
    areas = area_size * span
    owner = jnp.broadcast_to(owner_ref[...], (areas, rows_held))
    marks = jnp.where(owner == lax.broadcasted_iota(jnp.int32, owner.shape, 0), 1.0, 0.0)
    earlier_row = lax.broadcasted_iota(jnp.int32, (rows_held, rows_held), 0)
    this_row = lax.broadcasted_iota(jnp.int32, (rows_held, rows_held), 1)
    order = jnp.where(earlier_row < this_row, 1.0, 0.0).astype(BF16)
    marks_low = marks.astype(BF16)
    ahead = jnp.dot(marks_low, order, preferred_element_type=F32)
    rank = jnp.sum(ahead * marks, axis=0, keepdims=True)
    slot = owner_ref[...] * CAPACITY + rank.astype(jnp.int32)
    slots = areas * CAPACITY
    wide = jnp.broadcast_to(slot, (slots, rows_held))
    pick = jnp.where(wide == lax.broadcasted_iota(jnp.int32, wide.shape, 0), 1.0, 0.0).astype(BF16)

    def thirds(x):
        high = x.astype(BF16)
        rest = x - high.astype(F32)
        middle = rest.astype(BF16)
        return high, middle, (rest - middle.astype(F32)).astype(BF16)

    sens_load.wait()
    moved = [jnp.dot(pick, part, preferred_element_type=F32) for part in thirds(sens_own[...])]
    sens_out[...] = (moved[0] + moved[1] + moved[2]).reshape(area_size, per_device, 128)
    load_load.wait()
    loads = load_own[...]
    load_stack[...] = jnp.zeros_like(load_stack)
    load_stack[0:hours, :] = jnp.where(rank < 0.5, loads, 0.0)
    load_stack[64 : 64 + hours, :] = jnp.where(rank > 0.5, loads, 0.0)
    moved = [
        lax.dot_general(marks_low, part, NT, preferred_element_type=F32) for part in thirds(load_stack[...])
    ]
    load_out[...] = (moved[0] + moved[1] + moved[2]).reshape(area_size, span, 128)

    def piece(i, j):
        return pl.ds(j * span + i, hours, stride=span * parts)

    def columns(j):
        return slice(j * 128, (j + 1) * 128)

    raw_loads[0].wait()
    for i in range(span):
        guess_ref[i, padded - 8 : padded, :] = jnp.zeros((8, width), F32)
        for j in range(parts):
            guess_ref[i, 0:hours, columns(j)] = raw[0, piece(i, j), :]

    for copy in raw_loads[1:]:
        copy.wait()
    scale = barrier_ref[0]
    for i in range(span):
        diag_buf[i, padded - 8 : padded, :] = jnp.zeros((8, width), F32)
        right_ref[i, padded - 8 : padded, :] = jnp.zeros((8, width), F32)
        for j in range(parts):
            slack = raw[1, piece(i, j), :]
            diag_buf[i, 0:hours, columns(j)] = raw[2, piece(i, j), :] + scale / (slack * slack)
            right_ref[i, 0:hours, columns(j)] = scale / slack - raw[3, piece(i, j), :]

    tile_load.wait()
    for i in range(span):
        high, low = split(tile_buf[i])
        tile_high[i] = high
        tile_low[i] = low

    first = me_a * span

    def gains_of(start, valid):
        table = []
        for r in range(span):
            area = start + r
            row = []
            for o in range(1, TIES + 1):
                total = jnp.float32(0.0)
                for k in range(TIES):
                    total = total + jnp.where(tie_offset[k, area] == o, tie_gain[k, area], 0.0)
                inside = jnp.logical_and(valid, area + o < areas)
                row.append(jnp.where(inside, total, 0.0))
            table.append(row)
        return table

    lower_start = lax.rem(me_a + area_size - 1, area_size) * span
    window = gains_of(lower_start, me_a > 0) + gains_of(first, me_a >= 0)

    pl.semaphore_wait(barrier, greeted)

    def remote(source, target, send, recv, device):
        return pltpu.make_async_remote_copy(
            src_ref=source, dst_ref=target, send_sem=send, recv_sem=recv,
            device_id=device, device_id_type=MESH,
        )

    steps = [0]
    for d in range(1, (zeds + 1) // 2):
        steps += [d, -d]
    if zeds % 2 == 0:
        steps += [zeds // 2]
    steps = [d % zeds for d in steps]
    own_rows = pl.ds(pl.multiple_of(me_a * per_device, per_device), per_device)
    block_copies, load_copies = {}, {}
    for dz in steps:
        for e in range(plane):
            to = lax.rem(zed + dz, zeds) * plane + lax.rem(place + e, plane)
            key = ((zeds - dz) % zeds) * plane + (plane - e) % plane
            if dz == 0 and e == 0:
                block = pltpu.make_async_copy(sens_out.at[me_a], sens_got.at[me_t, own_rows], sens_recv.at[key])
                load = pltpu.make_async_copy(load_out.at[me_a], load_got.at[me_a], load_recv.at[key])
            else:
                block = remote(
                    sens_out.at[to], sens_got.at[me_t, own_rows], sens_send.at[key], sens_recv.at[key], (me_t, to)
                )
                load = remote(load_out.at[to], load_got.at[me_a], load_send.at[key], load_recv.at[key], (me_t, to))
            block.start()
            block_copies[key] = block
            load_copies[key] = load

    for copy in load_copies.values():
        copy.start()
    coup_copies = [
        remote(coup_ref, coup_halo.at[0], coup_send.at[0], coup_recv.at[0], above),
        remote(coup_ref, coup_halo.at[1], coup_send.at[1], coup_recv.at[1], below),
    ]
    for copy in coup_copies:
        copy.start()

    def stage_hours(phase, source):
        for i in range(span):
            hour_stage[phase, 0, i : i + 1, :] = source[i, 0:1, :]
            hour_stage[phase, 1, i : i + 1, :] = source[i, hours - 1 : hours, :]

    def send_area(phase, source, side, i):
        copy = remote(
            source.at[i], halo.at[phase, side, i], halo_send.at[phase, side, i], halo_recv.at[phase, side, i],
            below if side else above,
        )
        copy.start()
        flying[phase][side, i] = copy

    def hour_copies(phase):
        return [
            remote(hour_stage.at[phase, 1], hour_halo.at[phase, 0], hour_send.at[phase, 0], hour_recv.at[phase, 0], later),
            remote(hour_stage.at[phase, 0], hour_halo.at[phase, 1], hour_send.at[phase, 1], hour_recv.at[phase, 1], earlier),
        ]

    def send_hours(phase, source):
        stage_hours(phase, source)
        for side, copy in enumerate(hour_copies(phase)):
            copy.start()
            flying[phase]["hours", side] = copy

    ready = (1, 2, 0, 3)
    sends = {1: [(1, 1)], 2: [(0, 2), (0, 1), (1, 2)], 0: [(1, 0)], 3: [(0, 3), (0, 0), (1, 3)]}
    flying = [{}, {}, {}]
    send_hours(0, guess_ref)
    for i in ready:
        for side, j in sends[i]:
            send_area(0, guess_ref, side, j)

    offsets = [o for o in range(-TIES, TIES + 1) if o != 0]

    def tile_part(value, i):
        high, low = split(value)
        stacked = jnp.concatenate([high, low], axis=0)
        return product(stacked, high, tile_high[i], tile_low[i], NN)

    def security_part(value, i):
        high, low = split(value)
        stacked = jnp.concatenate([high, low], axis=0)
        flow = product(stacked, high, sens_high[i], sens_low[i], NT) * weight_ref[i]
        flow_high, flow_low = split(flow)
        flow_stacked = jnp.concatenate([flow_high, flow_low], axis=0)
        return product(flow_stacked, flow_high, sens_high[i], sens_low[i], NN)

    def local_part(value, i):
        return tile_part(value, i) + security_part(value, i)

    rows = lax.broadcasted_iota(jnp.int32, (padded, width), 0)
    first_hours = me_t == 0
    last_hours = me_t == tm_size - 1

    def near_part(source, i):
        value = source[i]
        beside = pltpu.roll(value, padded - 1, 0) + pltpu.roll(value, 1, 0)
        beside = jnp.where(rows < hours, beside, jnp.zeros_like(beside))
        out = acc[i] + diag_buf[i] * value - ramp_ref[i : i + 1, :] * beside
        for k, o in enumerate(offsets):
            if 0 <= i + o < span:
                out = out - tie_buf[i, k : k + 1, :] * source[i + o]
        acc[i] = out

    def hour_part(phase):
        for side in range(2):
            flying[phase]["hours", side].wait_recv()
        for i in range(span):
            ramp = ramp_ref[i : i + 1, :]
            before = ramp * hour_halo[phase, 0, i : i + 1, :]
            after = ramp * hour_halo[phase, 1, i : i + 1, :]
            acc[i, 0:1, :] = acc[i, 0:1, :] - jnp.where(first_hours, jnp.zeros_like(before), before)
            acc[i, hours - 1 : hours, :] = acc[i, hours - 1 : hours, :] - jnp.where(
                last_hours, jnp.zeros_like(after), after
            )

    def halo_part(phase, pieces):
        for piece_key in pieces:
            flying[phase][piece_key].wait_recv()
        for i in range(span):
            terms = []
            for side, j in pieces:
                o = span + j - i if side else j - span - i
                if abs(o) <= TIES:
                    k = offsets.index(o)
                    terms.append(tie_buf[i, k : k + 1, :] * halo[phase, side, j])
            if terms:
                acc[i] = acc[i] - functools.reduce(lambda x, y: x + y, terms)

    pieces_one = [(0, 2), (1, 1)]
    pieces_two = [(0, 1), (1, 2)]
    pieces_three = [(0, 3), (1, 0)]
    pieces_four = [(0, 0), (1, 3)]

    group = plane * per_device
    passes, relays = [], []

    def group_rows(k):
        z = lax.rem(zed + steps[k], zeds)
        return pl.ds(pl.multiple_of(z * group, group), group)

    def relay(k):
        forward = k % 2 == 0
        passes[k][0 if forward else 1].wait_recv()
        origin = lax.rem(me_t + (tm_size - 1 if forward else 1), tm_size)
        there = sens_got.at[origin, group_rows(k)]
        copy = remote(there, there, relay_send.at[k], pass_recv.at[k, 2], later if forward else earlier)
        copy.start()
        relays.append(copy)

    def go_round(k):
        for e in range(plane):
            key = steps[k] * plane + e
            if key == 0:
                block_copies[key].wait()
            else:
                block_copies[key].wait_recv()
        here = sens_got.at[me_t, group_rows(k)]
        pair = [
            remote(here, here, pass_send.at[k, 0], pass_recv.at[k, 0], later),
            remote(here, here, pass_send.at[k, 1], pass_recv.at[k, 1], earlier),
        ]
        for copy in pair:
            copy.start()
        passes.append(pair)
        if k >= 1:
            relay(k - 1)

    go_round(0)
    go_round(1)
    for copy in coup_copies:
        copy.wait()
    coupling = [coup_halo[0, i : i + 1, :] for i in range(span)]
    coupling += [coup_ref[i : i + 1, :] for i in range(span)]
    coupling += [coup_halo[1, i : i + 1, :] for i in range(span)]
    for i in range(span):
        total = 2.0 * ramp_ref[i : i + 1, :]
        for k, o in enumerate(offsets):
            gain = window[span + i][o - 1] if o > 0 else window[span + i + o][-o - 1]
            row = coupling[span + i] * coupling[span + i + o] * gain
            tie_buf[i, k : k + 1, :] = row
            total = total + row
        diag_buf[i] = diag_buf[i] + total

    go_round(2)
    acc[0] = tile_part(guess_ref[0], 0)
    near_part(guess_ref, 0)
    go_round(3)
    acc[1] = tile_part(guess_ref[1], 1)
    near_part(guess_ref, 1)
    go_round(4)
    acc[2] = tile_part(guess_ref[2], 2)
    near_part(guess_ref, 2)
    go_round(5)
    acc[3] = tile_part(guess_ref[3], 3)
    near_part(guess_ref, 3)
    go_round(6)
    go_round(7)
    relay(zeds - 1)

    for key, copy in load_copies.items():
        if key == 0:
            copy.wait()
        else:
            copy.wait_recv()
    for i in range(span):
        seen = load_got[:, i, :].T
        weight_ref[i] = jnp.concatenate([seen[0:padded], seen[64 : 64 + padded]], axis=1)
    def place_columns(origin):
        where = pl.ds(pl.multiple_of(origin * 128, 128), 128)
        for i in range(span):
            for c in range(CAPACITY):
                high, low = split(sens_got[origin, pl.ds(i * CAPACITY + c, area_size, stride=per_device), :])
                sens_high[i, c * area_size : (c + 1) * area_size, where] = high
                sens_low[i, c * area_size : (c + 1) * area_size, where] = low

    place_columns(me_t)
    hour_part(0)
    for pieces in (pieces_one, pieces_two, pieces_three, pieces_four):
        halo_part(0, pieces)
    for k in range(zeds):
        passes[k][1 if k % 2 == 0 else 0].wait_recv()
    place_columns(lax.rem(me_t + tm_size - 1, tm_size))
    place_columns(lax.rem(me_t + 1, tm_size))
    for k in range(zeds):
        relays[k].wait_recv()
    place_columns(lax.rem(me_t + 2, tm_size))

    def start_stage(which, stage):
        copies = []
        for d in range(1, counts[stage]):
            to = lax.rem(mine[stage] + d, counts[stage])
            copy = remote(
                red_stage.at[which, stage], red_slots.at[which, stage, mine[stage]],
                red_send.at[which, stage, d], red_recv.at[which, stage, d], partner(stage, to),
            )
            copy.start()
            copies.append(copy)
        return copies

    def end_stage(which, stage, copies):
        for copy in copies:
            copy.wait()
        total = jnp.zeros((1, 128), F32)
        for s in range(counts[stage]):
            total = total + red_slots[which, stage, s]
        return total

    def begin(which, stage, tile):
        red_stage[which, stage] = tile
        red_slots[which, stage, mine[stage]] = tile
        return start_stage(which, stage)

    lanes = lax.broadcasted_iota(jnp.int32, (1, 128), 1)

    def pack(values):
        total = jnp.zeros((1, 128), F32)
        for k, value in enumerate(values):
            total = jnp.where(lanes == k, jnp.sum(value, axis=1, keepdims=True), total)
        return total

    def take(total, k):
        return jnp.sum(jnp.where(lanes == k, total, jnp.zeros_like(total)), axis=1, keepdims=True)

    sum_rr = jnp.zeros((1, 128), F32)
    for i in ready:
        value = right_ref[i] - (acc[i] + security_part(guess_ref[i], i))
        field[0, i] = value
        for side, j in sends[i]:
            send_area(1, field.at[0], side, j)
        sum_rr = sum_rr + lane_sum(value * value)
    send_hours(1, field.at[0])
    for i in ready:
        acc[i] = local_part(field[0, i], i)
        near_part(field.at[0], i)
    sum_rv = jnp.zeros((1, 128), F32)
    halo_part(1, pieces_one)
    halo_part(1, pieces_two)
    hour_part(1)
    halo_part(1, pieces_three)
    for i in ready[:2]:
        field[1, i] = acc[i]
        for side, j in sends[i]:
            send_area(2, field.at[1], side, j)
    for i in ready[:2]:
        sum_rv = sum_rv + lane_sum(field[1, i] * field[0, i])
    acc[ready[0]] = local_part(field[1, ready[0]], ready[0])
    for piece_key in pieces_four:
        flying[1][piece_key].wait_recv()
    for i, (side, j) in zip(ready[2:], pieces_four):
        k = offsets.index(span + j - i if side else j - span - i)
        field[1, i] = acc[i] - tie_buf[i, k : k + 1, :] * halo[1, side, j]
        for side, j in sends[i]:
            send_area(2, field.at[1], side, j)
    send_hours(2, field.at[1])
    for i in ready[2:]:
        sum_rv = sum_rv + lane_sum(field[1, i] * field[0, i])
    copies = begin(0, 0, pack([sum_rr, sum_rv]))
    for i in ready[1:3]:
        acc[i] = local_part(field[1, i], i)
    total = end_stage(0, 0, copies)
    copies = begin(0, 1, total)
    acc[ready[3]] = local_part(field[1, ready[3]], ready[3])
    for i in ready:
        near_part(field.at[1], i)
    halo_part(2, pieces_one)
    halo_part(2, pieces_two)
    total = end_stage(0, 1, copies)
    rr_zero, rv_zero = take(total, 0), take(total, 1)
    alpha_zero = rr_zero / rv_zero
    for i in ready:
        right_ref[i] = guess_ref[i] + alpha_zero * field[0, i]
    hour_part(2)
    halo_part(2, pieces_three)

    sums = [jnp.zeros((1, 128), F32) for _ in range(4)]
    for i in ready:
        if i == ready[2]:
            halo_part(2, pieces_four)
        zero, one, two = field[0, i], field[1, i], acc[i]
        resid = zero - alpha_zero * one
        image = one - alpha_zero * two
        field[2, i] = image
        acc[i] = resid
        sums[0] = sums[0] + lane_sum(resid * resid)
        sums[1] = sums[1] + lane_sum(resid * image)
        sums[2] = sums[2] + lane_sum(resid * one)
        sums[3] = sums[3] + lane_sum(zero * image)
    copies = begin(1, 0, pack(sums))
    total = end_stage(1, 0, copies)
    copies = begin(1, 1, total)
    total = end_stage(1, 1, copies)
    rr_one = take(total, 0)
    beta = rr_one / rr_zero
    bend = take(total, 1) + beta * (take(total, 2) + take(total, 3)) + beta * beta * rv_zero
    alpha_one = rr_one / bend
    for i in range(span):
        resid = acc[i]
        zero = field[0, i]
        step = right_ref[i] + alpha_one * (resid + beta * zero)
        final = resid - alpha_one * (field[2, i] + beta * field[1, i])
        for j in range(parts):
            step_ref[piece(i, j), :] = step[0:hours, columns(j)]
            resid_ref[piece(i, j), :] = final[0:hours, columns(j)]
    for key in range(1, area_size):
        block_copies[key].wait_send()
        load_copies[key].wait_send()
    for k in range(zeds):
        for copy in passes[k]:
            copy.wait_send()
        relays[k].wait_send()
    for group_copies in flying:
        for copy in group_copies.values():
            copy.wait_send()


def deliver(step_ref, resid_ref, step_out, resid_out):
    step_out[...] = step_ref[...]
    resid_out[...] = resid_ref[...]


def body(
    gradient, barrier, slack, hess_diag, tile, ramp_weight, bus_coupling, tie_offset, tie_admittance,
    con_sens, con_weight, con_owner, step_guess,
):
    hours, span, width = gradient.shape
    tm_size, area_size = lax.axis_size("tm"), lax.axis_size("area")
    rows_held = con_sens.shape[0]
    parts = width // 128
    padded = -(-hours // 8) * 8
    per_device = span * CAPACITY
    zeds = area_size // (Y_SIZE * CORES)
    most = max(tm_size * Y_SIZE, area_size // Y_SIZE)
    own_slots = area_size * CAPACITY

    def rows_of(x):
        return jnp.transpose(x.reshape(hours, span, parts, 128), (0, 2, 1, 3)).reshape(hours * parts * span, 128)

    def field_of(x):
        return jnp.transpose(x.reshape(hours, parts, span, 128), (0, 2, 1, 3)).reshape(hours, span, width)

    vmem = pl.BlockSpec(memory_space=pltpu.VMEM)
    smem = pl.BlockSpec(memory_space=pltpu.SMEM)
    anywhere = pl.BlockSpec(memory_space=pl.ANY)
    dma = pltpu.SemaphoreType.DMA
    flat = jax.ShapeDtypeStruct((hours * parts * span, 128), F32)
    block = (span, padded, width)
    step, residual = pl.pallas_call(
        functools.partial(kernel, hours, tm_size, area_size),
        out_shape=(flat, flat),
        in_specs=[smem] * 3 + [anywhere] * 5 + [vmem] * 2 + [anywhere] * 2 + [vmem],
        out_specs=(vmem, vmem),
        scratch_shapes=[
            pltpu.VMEM((4,) + flat.shape, F32),
            pltpu.VMEM(block, F32), pltpu.VMEM(block, F32), pltpu.VMEM(block, F32),
            pltpu.VMEM(tile.shape, F32), pltpu.VMEM(tile.shape, BF16), pltpu.VMEM(tile.shape, BF16),
            pltpu.VMEM((rows_held, 128), F32), pltpu.VMEM((hours, rows_held), F32), pltpu.VMEM((128, rows_held), F32),
            pltpu.VMEM((area_size, per_device, 128), F32), pltpu.VMEM((area_size, span, 128), F32),
            pltpu.VMEM((parts, area_size * per_device, 128), F32), pltpu.VMEM((area_size, span, 128), F32),
            pltpu.VMEM((span, own_slots, width), BF16), pltpu.VMEM((span, own_slots, width), BF16),
            pltpu.VMEM((span, padded, own_slots), F32),
            pltpu.VMEM((span, 2 * TIES, width), F32),
            pltpu.VMEM((3,) + block, F32),
            pltpu.VMEM(block, F32),
            pltpu.VMEM((3, 2) + block, F32),
            pltpu.VMEM((3, 2, span, width), F32), pltpu.VMEM((3, 2, span, width), F32), pltpu.VMEM((2, span, width), F32),
            pltpu.VMEM((2, 2, 1, 128), F32), pltpu.VMEM((2, 2, most, 1, 128), F32),
            dma((7,)), dma((3, 2, span)), dma((3, 2, span)), dma((3, 2)), dma((3, 2)), dma((2,)), dma((2,)),
            dma((2, 2, most)), dma((2, 2, most)),
            dma((area_size,)), dma((area_size,)), dma((area_size,)), dma((area_size,)),
            dma((zeds, 2)), dma((zeds, 3)), dma((zeds,)),
        ],
        compiler_params=pltpu.CompilerParams(collective_id=0, has_side_effects=True, vmem_limit_bytes=60 * 1024 * 1024),
    )(
        barrier, tie_offset.T, tie_admittance.T, rows_of(slack), rows_of(hess_diag), rows_of(gradient),
        rows_of(step_guess), tile, ramp_weight, bus_coupling, con_sens, con_weight.T, con_owner.T,
    )
    step, residual = pl.pallas_call(
        deliver, out_shape=(flat, flat), in_specs=[vmem, vmem], out_specs=(vmem, vmem),
    )(step, residual)
    return field_of(step), field_of(residual)


def solution(mesh):
    placed = (
        P("tm", "area", None), P(), P("tm", "area", None), P("tm", "area", None), P("area", None, None),
        P("area", None), P("area", None), P(), P(), P("area", None), P("area", "tm"), P("area", None),
        P("tm", "area", None),
    )
    return jax.shard_map(
        body, mesh=mesh, in_specs=placed,
        out_specs=(P("tm", "area", None), P("tm", "area", None)), check_vma=False,
    )
```
